32 devices in a mesh: section: 2 (over core), dp: 16 (over z, y, x).
Axes of the slice: x: 2, y: 2, z: 4, core: 2. Of those that a mesh axis runs over, the one named last changes fastest.
Arguments:
- node_table: bfloat16 [128, 2048], replicated, may hold values from -60 to 60
- tiles: int32 [4, 512], P(None, 'dp'), may hold values from 0 to 96
- neighbours: int32 [4, 512, 8], P(None, 'dp'), may hold values from 0 to 31
- distances: float32 [4, 512, 8], P(None, 'dp'), may hold values from 0 to 0.9
- proj: bfloat16 [2, 2048, 512], P('section'), may hold values from -0.125 to 0.125
- upstream: bfloat16 [4, 512, 2048], P(None, 'dp'), may hold values from -6 to 6
Outputs:
- grad: float32 [2, 2048, 512], P('section', 'dp')
The draws below stay inside these ranges and needn't reach their ends.
All inputs are finite; a program needn't handle non-finite values.
Results may differ from the reference program's by a relative error of at most 0.024.
Values may be sent and summed in bfloat16 or wider, within the bound.
No kernel may reach another device: no remote copies, remote signals or barrier semaphores. Data moves between devices by JAX's collectives and lax.ppermute only.
A program may use at most 64 MiB of HBM per device.

```python
import math
import jax
import jax.numpy as jnp
from jax import lax

D = 2048
RANK = 512
MICRO = 4
NODES = 128
LOCAL = 32
NEIGH = 8
SECTIONS = 2
POINTS = 512


def draw_node_table(key, part):
    key_base = jax.random.fold_in(key, 11)
    key_values, key_rows, key_cols = jax.random.split(key_base, 3)
    row_scale = jnp.exp(jax.random.uniform(key_rows, (NODES, 1), jnp.float32, math.log(0.4), math.log(4.0)))
    col_scale = jnp.exp(jax.random.uniform(key_cols, (1, D), jnp.float32, math.log(0.5), math.log(2.0)))
    values = jax.random.normal(key_values, (NODES, D), jnp.float32)
    table = jnp.clip(values * row_scale * col_scale, -60.0, 60.0)
    return table.astype(jnp.bfloat16)


def with_ends(drawn, key, least, high):
    index_at = [jax.random.randint(jax.random.fold_in(key, axis), (), 0, length) for axis, length in enumerate(drawn.shape)]
    main_axis = drawn.shape.index(max(drawn.shape))
    next_to = index_at[:main_axis] + [(index_at[main_axis] + 1) % drawn.shape[main_axis]] + index_at[main_axis + 1:]
    return drawn.at[tuple(index_at)].set(least).at[tuple(next_to)].set(high)


def with_spikes(entries, own_key, source, target, parts, factor):
    def block_of(axis_at):
        return (jnp.arange(entries.shape[axis_at]) // (entries.shape[axis_at] // parts)).reshape((-1,) + (1,) * (entries.ndim - 1 - axis_at))

    first = jax.random.permutation(own_key, parts)[block_of(target)]
    other_side = (block_of(target) + parts // 2) % parts
    return jnp.where((block_of(source) == first) | (block_of(source) == other_side), factor * entries, entries)


def levels(key, dims, cuts, low, high):
    factor_of = 1.0
    for position, parts in cuts:
        steps = jax.random.uniform(jax.random.fold_in(jax.random.fold_in(key, 6), position), (parts,), jnp.float32, low / len(cuts), high / len(cuts))
        factor_of = factor_of * jnp.repeat(jnp.exp(steps), dims[position] // parts).reshape((-1,) + (1,) * (len(dims) - 1 - position))
    return factor_of


def bell_draw(rng, dims, spread, reach, cuts=(), held_as=jnp.bfloat16):
    values = jax.random.normal(rng, dims, jnp.float32) * spread
    if len(cuts) > 0:
        values = levels(rng, dims, cuts, -0.22, 0.18) * values
    return jnp.clip(values, min=-reach, max=reach).astype(held_as)


def gaussian_with(rng, extent, scale, most, cuts, heavy, held_as=jnp.bfloat16):
    result = scale * jax.random.normal(rng, extent, jnp.float32)
    if cuts:
        result = result * levels(rng, extent, cuts, -0.22, 0.18)
    return jnp.clip(with_spikes(result, jax.random.fold_in(rng, 3), *heavy), -most, most).astype(held_as)


def setup_inputs(seed: int = 0) -> dict:
    seeds = jax.random.split(jax.random.key(seed), 7)
    node_table = draw_node_table(jax.random.fold_in(seeds[6], 71), 0)
    tiles = with_ends(jax.random.randint(seeds[1], (MICRO, POINTS), 0, NODES - LOCAL + 1), jax.random.fold_in(seeds[1], 1), 0, NODES - LOCAL).astype(jnp.int32)
    neighbours = with_ends(jax.random.randint(seeds[2], (MICRO, POINTS, NEIGH), 0, LOCAL), jax.random.fold_in(seeds[2], 1), 0, LOCAL - 1).astype(jnp.int32)
    distances = jnp.clip(0.9 * jax.random.uniform(seeds[3], (MICRO, POINTS, NEIGH), jnp.float32) ** levels(seeds[3], (MICRO, POINTS, NEIGH), ((1, 16),), -0.2, 0.2), 0.0, 0.9)
    proj = bell_draw(seeds[4], (SECTIONS, D, RANK), D ** -0.5, 0.125, ((0, 2),))
    upstream = gaussian_with(seeds[5], (MICRO, POINTS, D), 1.0, 6.0, ((1, 16),), (1, 2, 16, 2.0))
    return dict(node_table=node_table, tiles=tiles, neighbours=neighbours, distances=distances, proj=proj, upstream=upstream)


epsilon = 1e-05

def normalize(stream):
    wide = stream.astype(jnp.float32)
    inv_rms = lax.rsqrt(lax.optimization_barrier(jnp.mean(wide * wide, axis=-1, keepdims=True)) + epsilon)
    return (wide * inv_rms, inv_rms)

def contract_rows(left, right):
    return lax.dot_general(left, right, (((0,), (0,)), ((), ())), preferred_element_type=jnp.float32)

def contract_last(left, right):
    return lax.dot_general(left, right, (((1,), (1,)), ((), ())), preferred_element_type=jnp.float32)

def features(node_table, tile_row, neighbour_rows, distance_rows):
    kernel = (1.0 - distance_rows) ** 3 * (1.0 + 3.0 * distance_rows)
    weight_sum = lax.optimization_barrier(jnp.sum(kernel, axis=-1))
    node_index = (tile_row[:, None] + neighbour_rows).astype(jnp.int32)
    picked = jnp.take(node_table, node_index, axis=0).astype(jnp.float32)
    mixed = lax.optimization_barrier(jnp.sum(picked * kernel[:, :, None], axis=1)) / weight_sum[:, None]
    return mixed.astype(jnp.bfloat16)

def reference(node_table, tiles, neighbours, distances, proj, upstream):
    layers = proj.shape[0]

    def micro_step(totals, batch):
        tile_row, neighbour_rows, distance_rows, upstream_rows = batch
        stream = features(node_table, tile_row, neighbour_rows, distance_rows)
        inputs = []
        for layer in range(layers):
            inputs.append(stream)
            wide, inv_rms = normalize(stream)
            normed = wide.astype(jnp.bfloat16)
            hidden = jnp.tanh(jnp.dot(normed, proj[layer], preferred_element_type=jnp.float32)).astype(jnp.bfloat16)
            stream = (stream.astype(jnp.float32) + contract_last(hidden, proj[layer])).astype(jnp.bfloat16)
        grads = []
        cotangent = upstream_rows
        for layer in reversed(range(layers)):
            wide, inv_rms = normalize(inputs[layer])
            normed = wide.astype(jnp.bfloat16)
            hidden = jnp.tanh(jnp.dot(normed, proj[layer], preferred_element_type=jnp.float32)).astype(jnp.bfloat16)
            hidden_wide = hidden.astype(jnp.float32)
            grad_hidden = jnp.dot(cotangent, proj[layer], preferred_element_type=jnp.float32)
            grad_act = (grad_hidden * (1.0 - hidden_wide * hidden_wide)).astype(jnp.bfloat16)
            grad_norm = contract_last(grad_act, proj[layer])
            grads.append(contract_rows(normed, grad_act) + contract_rows(cotangent, hidden))
            correction = lax.optimization_barrier(jnp.mean(grad_norm * wide, axis=-1, keepdims=True))
            cotangent = (cotangent.astype(jnp.float32) + inv_rms * (grad_norm - wide * correction)).astype(jnp.bfloat16)
        return (totals + jnp.stack(grads[::-1]), None)
    zeros = jnp.zeros(proj.shape, jnp.float32)
    grad, _ = lax.scan(micro_step, zeros, (tiles, neighbours, distances, upstream))
    factor = 1.0 / math.sqrt(MICRO * POINTS)
    return grad * factor
```

```python
import functools
import itertools
import math

import jax
import jax.numpy as jnp
from jax import lax
from jax.experimental import pallas as pl
from jax.experimental.pallas import tpu as pltpu
from jax.sharding import PartitionSpec as P


epsilon = 1e-05
AXES = ("section", "dp")
SHARED_BITS = (2, 0)
WIDE = 512


def mask_of(number, bits):
    return sum(((number >> i) & 1) << bit for i, bit in enumerate(bits))


class Plan:
    def __init__(self, sections, replicas, points):
        self.sections, self.replicas, self.points = sections, replicas, points
        bits = replicas.bit_length() - 1
        self.shared = tuple(bit for bit in SHARED_BITS if bit < bits)
        self.summed = tuple(bit for bit in (1, 3, *range(bits)) if bit < bits and bit not in self.shared)
        self.summed = tuple(dict.fromkeys(self.summed))
        self.rows = (points << len(self.shared)) // sections
        self.unit = min(points, self.rows)
        self.units = self.rows // self.unit
        self.parts = points // self.unit
        self.blocks = 1 << len(self.summed)

    def order(self, section):
        turn = section % max(len(self.summed), 1)
        return self.summed[turn:] + self.summed[:turn]

    def source_mask(self, section, j):
        return mask_of((section * self.units + j) // self.parts, self.shared)


def permute(block, plan, route):
    pairs = []
    for section, replica in itertools.product(range(plan.sections), range(plan.replicas)):
        to_section, to_replica = route(section, replica)
        pairs.append((section * plan.replicas + replica, to_section * plan.replicas + to_replica))
    return lax.ppermute(block, AXES, pairs)


def dot(left, right, dims):
    return lax.dot_general(left, right, (dims, ((), ())), preferred_element_type=jnp.float32)


def weight_copies(plan, weights, held, sem):
    me = lax.axis_index("section")
    copies = []
    for turn in range(plan.sections):
        place = lax.rem(me + turn, plan.sections)
        copies.append(pltpu.make_async_copy(weights[turn].at[0], held.at[place], sem.at[turn]))
    return copies


def forward_kernel(plan, *refs):
    units, sections = plan.units, plan.sections
    small, refs = refs[:units], refs[units:]
    table, refs = refs[0], refs[1:]
    weights, refs = refs[:sections], refs[sections:]
    streams, hiddens, scales, held, total, normed, sem = refs
    copies = weight_copies(plan, weights, held, sem)
    for copy in copies:
        copy.start()
    unit, width = plan.unit, table.shape[1]
    nodes = table.shape[0]
    count = small[0].shape[0] // 2
    for j in range(units):
        rows = pl.ds(j * unit, unit)
        index = small[j][:count, :].astype(jnp.int32)
        distance = small[j][count:, :]
        kernel = (1.0 - distance) ** 3 * (1.0 + 3.0 * distance)
        weight_sum = jnp.sum(kernel, axis=0, keepdims=True)
        node = lax.broadcasted_iota(jnp.int32, (nodes, unit), 0)
        selector = jnp.zeros((nodes, unit), jnp.float32)
        for k in range(count):
            selector += jnp.where(node == index[k : k + 1, :], kernel[k : k + 1, :], 0.0)
        selector = selector / weight_sum
        high = selector.astype(jnp.bfloat16)
        low = (selector - high.astype(jnp.float32)).astype(jnp.bfloat16)
        squares = jnp.zeros((unit, 1), jnp.float32)
        for c in range(0, width, WIDE):
            columns = pl.ds(c, WIDE)
            value = dot(high, table[:, columns], ((0,), (0,))) + dot(low, table[:, columns], ((0,), (0,)))
            value = value.astype(jnp.bfloat16)
            streams[0, rows, columns] = value
            value = value.astype(jnp.float32)
            squares += jnp.sum(value * value, axis=1, keepdims=True)
        total[rows, :] = jnp.broadcast_to(squares, (unit, 128))
    for copy in copies:
        copy.wait()
    for s in range(sections):
        scale = lax.rsqrt(total[...][:, :1] * (1.0 / width) + epsilon)
        scales[s] = jnp.broadcast_to(scale, scales.shape[1:])
        for c in range(0, width, WIDE):
            columns = pl.ds(c, WIDE)
            normed[:, columns] = (streams[s, :, columns].astype(jnp.float32) * scale).astype(jnp.bfloat16)
        hidden = jnp.tanh(dot(normed[...], held[s], ((1,), (0,)))).astype(jnp.bfloat16)
        hiddens[s] = hidden
        if s + 1 == sections:
            break
        squares = jnp.zeros((plan.rows, 1), jnp.float32)
        for c in range(0, width, WIDE):
            columns = pl.ds(c, WIDE)
            value = streams[s, :, columns].astype(jnp.float32) + dot(hidden, held[s, columns, :], ((1,), (1,)))
            value = value.astype(jnp.bfloat16)
            streams[s + 1, :, columns] = value
            value = value.astype(jnp.float32)
            squares += jnp.sum(value * value, axis=1, keepdims=True)
        total[...] = jnp.broadcast_to(squares, (plan.rows, 128))


def backward_kernel(plan, *refs):
    units, sections = plan.units, plan.sections
    arrived, refs = refs[:units], refs[units:]
    streams, hiddens, scales = refs[:3]
    weights, refs = refs[3 : 3 + sections], refs[3 + sections :]
    kept, sent, refs = refs[0], refs[1] if sections > 1 else None, refs[2:] if sections > 1 else refs[1:]
    held, cotangent, norm_grad, left, right, share, sem = refs
    copies = weight_copies(plan, weights, held, sem)
    for copy in copies:
        copy.start()
    rows, unit, width = plan.rows, plan.unit, streams.shape[2]
    block = kept.shape[1]
    me = lax.axis_index("section")
    replica = lax.axis_index("dp")
    for j in range(units):
        cotangent[pl.ds(j * unit, unit), :] = arrived[j][...]
    for copy in copies:
        copy.wait()
    for s in reversed(range(sections)):
        scale = scales[s][:, :1]
        hidden = hiddens[s]
        wide_hidden = hidden.astype(jnp.float32)
        grad = dot(cotangent[...], held[s], ((1,), (0,))) * (1.0 - wide_hidden * wide_hidden)
        grad = grad.astype(jnp.bfloat16)
        right[:rows, :] = grad
        right[rows:, :] = hidden
        starts = [
            pl.multiple_of(jnp.bitwise_xor(replica, mask_of(number, plan.order(s)[::-1])) * block, block)
            for number in range(plan.blocks)
        ]
        if block % 128 == 0:
            reads = [(pl.ds(start, block), pl.ds(number * block, block)) for number, start in enumerate(starts)]
        else:
            reads = [(pl.ds(c, WIDE), pl.ds(c, WIDE)) for c in range(0, width, WIDE)]
        for columns, place in reads:
            left[:rows, place] = (streams[s, :, columns].astype(jnp.float32) * scale).astype(jnp.bfloat16)
            left[rows:, place] = cotangent[:, columns]
        share[...] = dot(left[...], right[...], ((0,), (0,)))
        turn = lax.rem(s + sections - me, sections)
        places = [pl.ds(number * block if block % 128 == 0 else start, block) for number, start in enumerate(starts)]

        @pl.when(turn == 0)
        def _():
            for number, place in enumerate(places):
                kept[number] = share[place, :]

        if sections > 1:

            @pl.when(turn > 0)
            def _():
                for number, place in enumerate(places):
                    sent[turn - 1, number] = share[place, :].astype(jnp.bfloat16)

        if s == 0:
            break
        correction = jnp.zeros((rows, 1), jnp.float32)
        for c in range(0, width, WIDE):
            columns = pl.ds(c, WIDE)
            value = dot(grad, held[s, columns, :], ((1,), (1,)))
            norm_grad[:, columns] = value
            wide = streams[s, :, columns].astype(jnp.float32) * scale
            correction += jnp.sum(value * wide, axis=1, keepdims=True)
        correction = correction * (1.0 / width)
        for c in range(0, width, WIDE):
            columns = pl.ds(c, WIDE)
            wide = streams[s, :, columns].astype(jnp.float32) * scale
            value = cotangent[:, columns].astype(jnp.float32) + scale * (norm_grad[:, columns] - wide * correction)
            cotangent[:, columns] = value.astype(jnp.bfloat16)


def on_device(node_table, tiles, neighbours, distances, proj, upstream):
    sections, replicas = lax.axis_size("section"), lax.axis_size("dp")
    micro_count, row_count, near = distances.shape
    nodes, width = node_table.shape
    rank = proj.shape[2]
    points = micro_count * row_count
    plan = Plan(sections, replicas, points)
    rows, unit, block = plan.rows, plan.unit, width // replicas
    me = lax.axis_index("section")

    index = (tiles[:, None, :] + neighbours.transpose(0, 2, 1)).astype(jnp.float32)
    small = jnp.concatenate([index, distances.transpose(0, 2, 1)], axis=1)
    small = small.transpose(1, 0, 2).reshape(2 * near, points)
    flat_upstream = upstream.reshape(points, width)

    def part_of(array, axis, j):
        if plan.parts == 1:
            return array
        part = lax.rem(me * plan.units + j, plan.parts)
        return lax.dynamic_slice_in_dim(array, part * unit, unit, axis)

    def unit_route(j):
        return lambda section, replica: (section, replica ^ plan.source_mask(section, j))

    small_units = [permute(part_of(small, 1, j), plan, unit_route(j)) for j in range(plan.units)]
    weights = [proj]
    for turn in range(1, sections):
        weights.append(permute(proj, plan, lambda section, replica: ((section - turn) % sections, replica)))
    arrived = [permute(part_of(flat_upstream, 0, j), plan, unit_route(j)) for j in range(plan.units)]

    in_vmem = pl.BlockSpec(memory_space=pltpu.VMEM)
    anywhere = pl.BlockSpec(memory_space=pl.ANY)
    bf16, f32 = jnp.bfloat16, jnp.float32
    streams, hiddens, scales = pl.pallas_call(
        functools.partial(forward_kernel, plan),
        out_shape=(
            jax.ShapeDtypeStruct((sections, rows, width), bf16),
            jax.ShapeDtypeStruct((sections, rows, rank), bf16),
            jax.ShapeDtypeStruct((sections, rows, 128), f32),
        ),
        in_specs=[in_vmem] * (plan.units + 1) + [anywhere] * sections,
        out_specs=(in_vmem,) * 3,
        scratch_shapes=[
            pltpu.VMEM((sections, width, rank), bf16),
            pltpu.VMEM((rows, 128), f32),
            pltpu.VMEM((rows, width), bf16),
            pltpu.SemaphoreType.DMA((sections,)),
        ],
        cost_estimate=pl.CostEstimate(
            flops=4 * sections * rows * width * rank, bytes_accessed=6 * width * rank, transcendentals=rows * rank
        ),
        name="forward",
    )(*small_units, node_table, *weights)
    formed = plan.blocks * block if block % 128 == 0 else width
    shapes = [jax.ShapeDtypeStruct((plan.blocks, block, rank), f32)]
    if sections > 1:
        shapes.append(jax.ShapeDtypeStruct((sections - 1, plan.blocks, block, rank), bf16))
    outs = pl.pallas_call(
        functools.partial(backward_kernel, plan),
        out_shape=tuple(shapes),
        in_specs=[in_vmem] * (plan.units + 3) + [anywhere] * sections,
        out_specs=(in_vmem,) * len(shapes),
        scratch_shapes=[
            pltpu.VMEM((sections, width, rank), bf16),
            pltpu.VMEM((rows, width), bf16),
            pltpu.VMEM((rows, width), f32),
            pltpu.VMEM((2 * rows, formed), bf16),
            pltpu.VMEM((2 * rows, rank), bf16),
            pltpu.VMEM((formed, rank), f32),
            pltpu.SemaphoreType.DMA((sections,)),
        ],
        cost_estimate=pl.CostEstimate(
            flops=6 * sections * rows * width * rank, bytes_accessed=6 * width * rank, transcendentals=0
        ),
        name="backward",
    )(*arrived, streams, hiddens, scales, *weights)
    total = outs[0]
    for turn in range(1, sections):
        total = total + permute(
            outs[1][turn - 1], plan, lambda section, replica: ((section + turn) % sections, replica)
        ).astype(f32)
    left = plan.blocks
    stage = 0
    while left > 1:
        left //= 2

        def route(section, replica):
            return section, replica ^ (1 << plan.order(section)[stage])

        total = total[:left] + permute(total[left:].astype(bf16), plan, route).astype(f32)
        stage += 1
    return total * (1.0 / math.sqrt(points * replicas))


def solution(mesh):
    return jax.shard_map(
        on_device,
        mesh=mesh,
        in_specs=(
            P(),
            P(None, "dp"),
            P(None, "dp", None),
            P(None, "dp", None),
            P("section", None, None),
            P(None, "dp", None),
        ),
        out_specs=P("section", "dp", None),
        check_vma=False,
    )
```

```python
import functools
import itertools
import math

import jax
import jax.numpy as jnp
from jax import lax
from jax.experimental import pallas as pl
from jax.experimental.pallas import tpu as pltpu
from jax.sharding import PartitionSpec as P


epsilon = 1e-05
AXES = ("section", "dp")
SHARED_BITS = (2, 0)
LIMIT = 36 << 20


def mask_of(number, bits):
    return sum(((number >> i) & 1) << bit for i, bit in enumerate(bits))


class Plan:
    def __init__(self, sections, replicas, points):
        self.sections, self.replicas, self.points = sections, replicas, points
        bits = replicas.bit_length() - 1
        self.shared = tuple(bit for bit in SHARED_BITS if bit < bits)
        self.summed = tuple(bit for bit in (1, 3, *range(bits)) if bit < bits and bit not in self.shared)
        self.summed = tuple(dict.fromkeys(self.summed))
        self.rows = (points << len(self.shared)) // sections
        self.unit = min(points, self.rows)
        self.units = self.rows // self.unit
        self.parts = points // self.unit
        self.blocks = 1 << len(self.summed)

    def order(self, section):
        turn = section % max(len(self.summed), 1)
        return self.summed[turn:] + self.summed[:turn]

    def source_mask(self, section, j):
        return mask_of((section * self.units + j) // self.parts, self.shared)


def permute(block, plan, route):
    pairs = []
    for section, replica in itertools.product(range(plan.sections), range(plan.replicas)):
        to_section, to_replica = route(section, replica)
        pairs.append((section * plan.replicas + replica, to_section * plan.replicas + to_replica))
    return lax.ppermute(block, AXES, pairs)


def dot(left, right, dims):
    return lax.dot_general(left, right, (dims, ((), ())), preferred_element_type=jnp.float32)


CHUNK = 256


def chunks(width):
    size = CHUNK if width % CHUNK == 0 else width
    return [pl.ds(start, size) for start in range(0, width, size)]


def lanes(value):
    size = value.shape[1]
    tile = 128 if size % 128 == 0 else size
    return sum(value[:, start : start + tile] for start in range(0, size, tile))


def forward_kernel(plan, *refs):
    units, sections = plan.units, plan.sections
    small, refs = refs[:units], refs[units:]
    table, refs = refs[0], refs[1:]
    weights, refs = refs[:sections], refs[sections:]
    streams, hiddens, inputs, scales, held, twice, sem, table_sem = refs
    nodes, width = table.shape
    rank = held.shape[2]
    me = lax.axis_index("section")
    table_copies = [pltpu.make_async_copy(table, twice.at[pl.ds(i * nodes, nodes)], table_sem.at[i]) for i in range(2)]
    for copy in table_copies:
        copy.start()
    copies = []
    for turn in range(sections):
        place = lax.rem(me + turn, sections)
        copies.append(pltpu.make_async_copy(weights[turn].at[0], held.at[place], sem.at[turn]))
        copies[-1].start()
    count = small[0].shape[0] // 2
    selectors = []
    for j in range(units):
        index = small[j][:count, :].astype(jnp.int32)
        distance = small[j][count:, :]
        kernel = (1.0 - distance) ** 3 * (1.0 + 3.0 * distance)
        kernel = kernel / jnp.sum(kernel, axis=0, keepdims=True)
        node = lax.broadcasted_iota(jnp.int32, (nodes, plan.unit), 0)
        selector = jnp.zeros((nodes, plan.unit), jnp.float32)
        for k in range(count):
            selector += jnp.where(node == index[k : k + 1, :], kernel[k : k + 1, :], 0.0)
        high = selector.astype(jnp.bfloat16)
        low = (selector - high.astype(jnp.float32)).astype(jnp.bfloat16)
        selectors.append(jnp.concatenate([high, low], axis=0))
    selector = jnp.concatenate(selectors, axis=1) if units > 1 else selectors[0]
    for copy in table_copies:
        copy.wait()
    squares = 0.0
    for columns in chunks(width):
        value = dot(selector, twice[:, columns], ((0,), (0,))).astype(jnp.bfloat16)
        streams[0, :, columns] = value
        value = value.astype(jnp.float32)
        squares += lanes(value * value)
    for copy in copies:
        copy.wait()
    for s in range(sections):
        scale = lax.rsqrt(jnp.sum(squares, axis=1, keepdims=True) * (1.0 / width) + epsilon)
        scales[s] = jnp.broadcast_to(scale, scales.shape[1:])
        for columns in chunks(rank):
            value = dot(streams[s], held[s, :, columns], ((1,), (0,))) * scale
            inputs[s, :, columns] = value
            hiddens[s, :, columns] = jnp.tanh(value).astype(jnp.bfloat16)
        if s + 1 == sections:
            break
        squares = 0.0
        for columns in chunks(width):
            value = streams[s, :, columns].astype(jnp.float32) + dot(hiddens[s], held[s, columns, :], ((1,), (1,)))
            value = value.astype(jnp.bfloat16)
            streams[s + 1, :, columns] = value
            value = value.astype(jnp.float32)
            squares += lanes(value * value)


def backward_kernel(plan, *refs):
    units, sections = plan.units, plan.sections
    arrived, refs = refs[:units], refs[units:]
    streams, hiddens, inputs, scales, held = refs[:5]
    kept, refs = refs[5], refs[6:]
    sent, refs = (refs[0], refs[1:]) if sections > 1 else (None, refs)
    cotangent, grads, left, right, share, sem = refs
    rows, unit, width, rank = plan.rows, plan.unit, streams.shape[2], hiddens.shape[2]
    block = kept.shape[1]
    me = lax.axis_index("section")
    replica = lax.axis_index("dp")
    copies = []
    for j in range(units):
        copies.append(pltpu.make_async_copy(arrived[j], cotangent.at[0, pl.ds(j * unit, unit)], sem.at[j]))
        copies[-1].start()
    for copy in copies:
        copy.wait()
    whole_blocks = block % 128 == 0

    def hand_out(s, starts):
        turn = lax.rem(s + sections - me, sections)
        held_at = s if whole_blocks else 0
        places = [pl.ds(number * block if whole_blocks else start, block) for number, start in enumerate(starts)]

        @pl.when(turn == 0)
        def _():
            for number, place in enumerate(places):
                kept[number] = share[held_at, place, :]

        if sections > 1:

            @pl.when(turn > 0)
            def _():
                for number, place in enumerate(places):
                    sent[turn - 1, number] = share[held_at, place, :].astype(jnp.bfloat16)

    pending = []
    for s in reversed(range(sections)):
        now, later = (sections - 1 - s) % 2, (sections - s) % 2
        scale = scales[s][:, :1]
        correction = 0.0
        for columns in chunks(rank):
            hidden = hiddens[s, :, columns].astype(jnp.float32)
            value = dot(cotangent[now], held[s, :, columns], ((1,), (0,))) * (1.0 - hidden * hidden)
            grad = value.astype(jnp.bfloat16)
            grads[:, columns] = grad
            right[:rows, columns] = (value * scale).astype(jnp.bfloat16)
            correction += lanes(grad.astype(jnp.float32) * inputs[s, :, columns])
        right[rows:, :] = hiddens[s]
        starts = [
            pl.multiple_of(jnp.bitwise_xor(replica, mask_of(number, plan.order(s)[::-1])) * block, block)
            for number in range(plan.blocks)
        ]
        if whole_blocks:
            reads = [(pl.ds(start, block), pl.ds(number * block, block)) for number, start in enumerate(starts)]
        else:
            reads = [(columns, columns) for columns in chunks(width)]
        for columns, place in reads:
            left[:rows, place] = streams[s, :, columns]
            left[rows:, place] = cotangent[now, :, columns]
        for columns in chunks(rank):
            share[s if whole_blocks else 0, :, columns] = dot(left[...], right[:, columns], ((0,), (0,)))
        if whole_blocks:
            pending.append((s, starts))
        else:
            hand_out(s, starts)
        if s == 0:
            break
        correction = jnp.sum(correction, axis=1, keepdims=True) * (1.0 / width) * scale * scale
        for columns in chunks(width):
            value = dot(grads[...], held[s, columns, :], ((1,), (1,)))
            value = cotangent[now, :, columns].astype(jnp.float32) + scale * value
            value = value - correction * streams[s, :, columns].astype(jnp.float32)
            cotangent[later, :, columns] = value.astype(jnp.bfloat16)
    for s, starts in pending:
        hand_out(s, starts)


def on_device(node_table, tiles, neighbours, distances, proj, upstream):
    sections, replicas = lax.axis_size("section"), lax.axis_size("dp")
    micro_count, row_count, near = distances.shape
    nodes, width = node_table.shape
    rank = proj.shape[2]
    points = micro_count * row_count
    plan = Plan(sections, replicas, points)
    rows, unit, block = plan.rows, plan.unit, width // replicas
    me = lax.axis_index("section")

    index = (tiles[:, None, :] + neighbours.transpose(0, 2, 1)).astype(jnp.float32)
    small = jnp.concatenate([index, distances.transpose(0, 2, 1)], axis=1)
    small = small.transpose(1, 0, 2).reshape(2 * near, points)
    flat_upstream = upstream.reshape(points, width)

    def part_of(array, axis, j):
        if plan.parts == 1:
            return array
        part = lax.rem(me * plan.units + j, plan.parts)
        return lax.dynamic_slice_in_dim(array, part * unit, unit, axis)

    def unit_route(j):
        return lambda section, replica: (section, replica ^ plan.source_mask(section, j))

    def other_core(j):
        def route(section, replica):
            return plan.sections - 1 - section, replica ^ plan.source_mask(plan.sections - 1 - section, j)

        return route

    arrived = [permute(part_of(flat_upstream, 0, j), plan, unit_route(j)) for j in range(plan.units)]
    if plan.parts == 1:
        small_units = [permute(small, plan, other_core(j)) for j in range(plan.units)]
    else:
        small_units = [permute(part_of(small, 1, j), plan, unit_route(j)) for j in range(plan.units)]
    weights = [pltpu.with_memory_space_constraint(proj, pltpu.HBM)]
    for turn in range(1, sections):
        weights.append(permute(proj, plan, lambda section, replica: ((section - turn) % sections, replica)))

    in_vmem = pl.BlockSpec(memory_space=pltpu.VMEM)
    anywhere = pl.BlockSpec(memory_space=pl.ANY)
    bf16, f32 = jnp.bfloat16, jnp.float32
    formed = plan.blocks * block if block % 128 == 0 else width
    held_back = pl.pallas_call(
        functools.partial(forward_kernel, plan),
        out_shape=(
            pltpu.VMEM((sections, rows, width), bf16),
            pltpu.VMEM((sections, rows, rank), bf16),
            pltpu.VMEM((sections, rows, rank), f32),
            pltpu.VMEM((sections, rows, 128), f32),
            pltpu.VMEM((sections, width, rank), bf16),
        ),
        in_specs=[in_vmem] * plan.units + [anywhere] * (sections + 1),
        out_specs=(in_vmem,) * 5,
        scratch_shapes=[
            pltpu.VMEM((2 * nodes, width), bf16),
            pltpu.SemaphoreType.DMA((sections,)),
            pltpu.SemaphoreType.DMA((2,)),
        ],
        cost_estimate=pl.CostEstimate(
            flops=4 * sections * rows * width * rank, bytes_accessed=6 * width * rank, transcendentals=rows * rank
        ),
        compiler_params=pltpu.CompilerParams(vmem_limit_bytes=LIMIT),
        name="forward",
    )(*small_units, pltpu.with_memory_space_constraint(node_table, pltpu.HBM), *weights)
    shapes = [jax.ShapeDtypeStruct((plan.blocks, block, rank), f32)]
    if sections > 1:
        shapes.append(jax.ShapeDtypeStruct((sections - 1, plan.blocks, block, rank), bf16))
    outs = pl.pallas_call(
        functools.partial(backward_kernel, plan),
        out_shape=tuple(shapes),
        in_specs=[anywhere] * plan.units + [in_vmem] * 5,
        out_specs=(in_vmem,) * len(shapes),
        scratch_shapes=[
            pltpu.VMEM((2, rows, width), bf16),
            pltpu.VMEM((rows, rank), bf16),
            pltpu.VMEM((2 * rows, formed), bf16),
            pltpu.VMEM((2 * rows, rank), bf16),
            pltpu.VMEM((sections if block % 128 == 0 else 1, formed, rank), f32),
            pltpu.SemaphoreType.DMA((plan.units,)),
        ],
        cost_estimate=pl.CostEstimate(
            flops=6 * sections * rows * width * rank, bytes_accessed=6 * width * rank, transcendentals=0
        ),
        compiler_params=pltpu.CompilerParams(vmem_limit_bytes=LIMIT),
        name="backward",
    )(*arrived, *held_back)
    total = outs[0]
    for turn in range(1, sections):
        total = total + permute(
            outs[1][turn - 1], plan, lambda section, replica: ((section + turn) % sections, replica)
        ).astype(f32)
    left = plan.blocks
    stage = 0
    while left > 1:
        left //= 2

        def route(section, replica):
            return section, replica ^ (1 << plan.order(section)[stage])

        total = total[:left] + permute(total[left:].astype(bf16), plan, route).astype(f32)
        stage += 1
    return total * (1.0 / math.sqrt(points * replicas))


def solution(mesh):
    return jax.shard_map(
        on_device,
        mesh=mesh,
        in_specs=(
            P(),
            P(None, "dp"),
            P(None, "dp", None),
            P(None, "dp", None),
            P("section", None, None),
            P(None, "dp", None),
        ),
        out_specs=P("section", "dp", None),
        check_vma=False,
    )
```

```python
import functools
import itertools
import math

import jax
import jax.numpy as jnp
from jax import lax
from jax.experimental import pallas as pl
from jax.experimental.pallas import tpu as pltpu
from jax.sharding import PartitionSpec as P


epsilon = 1e-05
AXES = ("section", "dp")
SHARED_BITS = (2, 0)
LIMIT = 36 << 20


def mask_of(number, bits):
    return sum(((number >> i) & 1) << bit for i, bit in enumerate(bits))


class Plan:
    def __init__(self, sections, replicas, points):
        self.sections, self.replicas, self.points = sections, replicas, points
        bits = replicas.bit_length() - 1
        self.shared = tuple(bit for bit in SHARED_BITS if bit < bits)
        self.summed = tuple(bit for bit in (1, 3, *range(bits)) if bit < bits and bit not in self.shared)
        self.summed = tuple(dict.fromkeys(self.summed))
        self.rows = (points << len(self.shared)) // sections
        self.unit = min(points, self.rows)
        self.units = self.rows // self.unit
        self.parts = points // self.unit
        self.blocks = 1 << len(self.summed)
        self.loads = 1 if sections == 2 else sections
        self.held = 2 if sections == 2 else 1
        self.relayed = sections == 2 and len(self.shared) == 2 and points % 32 == 0

    def order(self, section):
        turn = section % max(len(self.summed), 1)
        return self.summed[turn:] + self.summed[:turn]

    def units_of(self, section):
        units = [divmod(section * self.units + j, self.parts) for j in range(self.units)]
        units = [(mask_of(number, self.shared), part) for number, part in units]
        return sorted(units, key=lambda unit: unit[0].bit_count() != 1)

    def source_mask(self, section, j):
        return self.units_of(section)[j][0]


def permute(block, plan, route):
    pairs = []
    for section, replica in itertools.product(range(plan.sections), range(plan.replicas)):
        to_section, to_replica = route(section, replica)
        pairs.append((section * plan.replicas + replica, to_section * plan.replicas + to_replica))
    return lax.ppermute(block, AXES, pairs)


def dot(left, right, dims):
    return lax.dot_general(left, right, (dims, ((), ())), preferred_element_type=jnp.float32)


CHUNK = 256


def chunks(width):
    size = CHUNK if width % CHUNK == 0 else width
    return [pl.ds(start, size) for start in range(0, width, size)]


def lanes(value):
    size = value.shape[1]
    tile = 128 if size % 128 == 0 else size
    return sum(value[:, start : start + tile] for start in range(0, size, tile))


def by_section(plan, weights, body):
    me = lax.axis_index("section")
    if plan.sections != 2:
        body(me, lambda s: weights[0].at[s])
        return
    for place in range(2):
        pl.when(me == place)(functools.partial(body, place, lambda s, place=place: weights[(s + place) % 2]))


def prepare_kernel(plan, *refs):
    (*arrays, upstream), small, refs = refs[:4], refs[4], refs[5:]
    halves, (*held, sem) = (refs[:2], refs[2:]) if plan.relayed else ((), refs)
    packed = [pltpu.make_async_copy(array, ref, sem.at[j]) for j, (array, ref) in enumerate(zip(arrays, held))]
    taken = []
    half = plan.points // 2
    for j, ref in enumerate(halves):
        place = pl.multiple_of((lax.axis_index("section") ^ j) * half, half)
        taken.append(pltpu.make_async_copy(upstream.at[pl.ds(place, half)], ref, sem.at[3 + j]))
    for copy in packed + taken:
        copy.start()
    for copy in packed:
        copy.wait()
    tiles, neighbours, distances = held
    micro_count, near, _ = neighbours.shape
    index = [(neighbours[m] + tiles[m : m + 1, :]).astype(jnp.float32) for m in range(micro_count)]
    small[:near, :] = jnp.concatenate(index, axis=1)
    small[near:, :] = jnp.concatenate([distances[m] for m in range(micro_count)], axis=1)
    for copy in taken:
        copy.wait()


def load_kernel(plan, table, *refs):
    weights, refs = refs[: plan.loads], refs[plan.loads :]
    twice, held, sem = refs
    nodes = table.shape[0]
    copies = [pltpu.make_async_copy(table, twice.at[pl.ds(i * nodes, nodes)], sem.at[i]) for i in range(2)]
    if plan.sections == 2:
        copies.append(pltpu.make_async_copy(weights[0].at[0], held, sem.at[2]))
    else:
        me = lax.axis_index("section")
        for turn, weight in enumerate(weights):
            place = lax.rem(me + turn, plan.sections)
            copies.append(pltpu.make_async_copy(weight.at[0], held.at[place], sem.at[2 + turn]))
    for copy in copies:
        copy.start()
    for copy in copies:
        copy.wait()


def forward_kernel(plan, *refs):
    units, sections = plan.units, plan.sections
    given = 3 if plan.relayed else units
    small, twice, refs = refs[:given], refs[given], refs[given + 1 :]
    weights, refs = refs[: plan.held], refs[plan.held :]
    streams, hiddens, inputs, scales, total = refs
    nodes, width = twice.shape[0] // 2, twice.shape[1]
    rank = hiddens.shape[2]
    me = lax.axis_index("section")
    count = small[0].shape[0] // 2
    packed = [ref[...] for ref in small]
    if plan.relayed:
        half = plan.unit // 2
        near, across, own = packed
        low_half = lax.broadcasted_iota(jnp.int32, own.shape, 1) < half
        mixed = jnp.where(low_half == (me == 0), own, across)
        packed = [jnp.where(me == 0, a, b) for a, b in ((near, pltpu.roll(near, half, 1)), (pltpu.roll(mixed, half, 1), mixed))]
    selectors = []
    for j in range(units):
        index = packed[j][:count, :].astype(jnp.int32)
        distance = packed[j][count:, :]
        kernel = (1.0 - distance) ** 3 * (1.0 + 3.0 * distance)
        kernel = kernel / jnp.sum(kernel, axis=0, keepdims=True)
        node = lax.broadcasted_iota(jnp.int32, (nodes, plan.unit), 0)
        selector = jnp.zeros((nodes, plan.unit), jnp.float32)
        for k in range(count):
            selector += jnp.where(node == index[k : k + 1, :], kernel[k : k + 1, :], 0.0)
        high = selector.astype(jnp.bfloat16)
        low = (selector - high.astype(jnp.float32)).astype(jnp.bfloat16)
        selectors.append(jnp.concatenate([high, low], axis=0))
    selector = jnp.concatenate(selectors, axis=1) if units > 1 else selectors[0]
    squares = 0.0
    for columns in chunks(width):
        value = dot(selector, twice[:, columns], ((0,), (0,))).astype(jnp.bfloat16)
        streams[0, :, columns] = value
        value = value.astype(jnp.float32)
        squares += lanes(value * value)
    total[...] = squares

    def body(me, weight_of):
        squares = total[...]
        for s in range(sections):
            weight = weight_of(s)
            scale = lax.rsqrt(jnp.sum(squares, axis=1, keepdims=True) * (1.0 / width) + epsilon)
            scales[s] = jnp.broadcast_to(scale, scales.shape[1:])
            for columns in chunks(rank):
                value = dot(streams[s], weight[:, columns], ((1,), (0,))) * scale
                inputs[s, :, columns] = value
                hiddens[s, :, columns] = jnp.tanh(value).astype(jnp.bfloat16)
            if s + 1 == sections:
                break
            squares = 0.0
            for columns in chunks(width):
                value = streams[s, :, columns].astype(jnp.float32) + dot(hiddens[s], weight[columns, :], ((1,), (1,)))
                value = value.astype(jnp.bfloat16)
                streams[s + 1, :, columns] = value
                value = value.astype(jnp.float32)
                squares += lanes(value * value)

    by_section(plan, weights, body)


def backward_kernel(plan, *refs):
    sections = plan.sections
    given = 4 if plan.relayed else plan.units
    arrived, refs = refs[:given], refs[given:]
    streams, hiddens, inputs, scales = refs[:4]
    weights, refs = refs[4 : 4 + plan.held], refs[4 + plan.held :]
    kept, refs = refs[0], refs[1:]
    sent, refs = (refs[0], refs[1:]) if sections > 1 else (None, refs)
    cotangent, grads, left, right, share = refs
    rows, width, rank = plan.rows, streams.shape[2], hiddens.shape[2]
    block = kept.shape[1]
    replica = lax.axis_index("dp")
    step = rows // len(arrived)
    for j, ref in enumerate(arrived):
        cotangent[0, pl.ds(j * step, step), :] = ref[...]
    whole_blocks = block % 128 == 0

    def hand_out(me, s, starts):
        turn = (s + sections - me) % sections if isinstance(me, int) else lax.rem(s + sections - me, sections)
        places = [pl.ds(number * block if whole_blocks else start, block) for number, start in enumerate(starts)]

        def keep():
            for number, place in enumerate(places):
                kept[number] = share[place, :]

        def send():
            for number, place in enumerate(places):
                sent[turn - 1, number] = share[place, :].astype(jnp.bfloat16)

        if isinstance(me, int):
            keep() if turn == 0 else send()
            return
        pl.when(turn == 0)(keep)
        if sections > 1:
            pl.when(turn > 0)(send)

    def body(me, weight_of):
        for s in reversed(range(sections)):
            weight = weight_of(s)
            now, later = (sections - 1 - s) % 2, (sections - s) % 2
            scale = scales[s][:, :1]
            correction = 0.0
            for columns in chunks(rank):
                hidden = hiddens[s, :, columns].astype(jnp.float32)
                value = dot(cotangent[now], weight[:, columns], ((1,), (0,))) * (1.0 - hidden * hidden)
                grad = value.astype(jnp.bfloat16)
                grads[:, columns] = grad
                right[:rows, columns] = (value * scale).astype(jnp.bfloat16)
                correction += lanes(grad.astype(jnp.float32) * inputs[s, :, columns])
            right[rows:, :] = hiddens[s]
            starts = [
                pl.multiple_of(jnp.bitwise_xor(replica, mask_of(number, plan.order(s)[::-1])) * block, block)
                for number in range(plan.blocks)
            ]
            if whole_blocks:
                reads = [(pl.ds(start, block), pl.ds(number * block, block)) for number, start in enumerate(starts)]
            else:
                reads = [(columns, columns) for columns in chunks(width)]
            for columns, place in reads:
                left[:rows, place] = streams[s, :, columns]
                left[rows:, place] = cotangent[now, :, columns]
            if s > 0:
                correction = jnp.sum(correction, axis=1, keepdims=True) * (1.0 / width) * scale * scale
                for columns in chunks(width):
                    value = dot(grads[...], weight[columns, :], ((1,), (1,)))
                    value = cotangent[now, :, columns].astype(jnp.float32) + scale * value
                    value = value - correction * streams[s, :, columns].astype(jnp.float32)
                    cotangent[later, :, columns] = value.astype(jnp.bfloat16)
            for columns in chunks(rank):
                share[:, columns] = dot(left[...], right[:, columns], ((0,), (0,)))
            hand_out(me, s, starts)

    by_section(plan, weights, body)


def on_device(node_table, tiles, neighbours, distances, proj, upstream):
    sections, replicas = lax.axis_size("section"), lax.axis_size("dp")
    micro_count, row_count, near = distances.shape
    nodes, width = node_table.shape
    rank = proj.shape[2]
    points = micro_count * row_count
    plan = Plan(sections, replicas, points)
    rows, unit, block = plan.rows, plan.unit, width // replicas
    me = lax.axis_index("section")

    in_vmem = pl.BlockSpec(memory_space=pltpu.VMEM)
    anywhere = pl.BlockSpec(memory_space=pl.ANY)
    bf16, f32 = jnp.bfloat16, jnp.float32
    in_hbm = functools.partial(pltpu.with_memory_space_constraint, memory_space=pltpu.HBM)
    flat_upstream = upstream.reshape(points, width)
    limit = pltpu.CompilerParams(vmem_limit_bytes=LIMIT)
    packs = [pltpu.VMEM((2 * near, points), f32)]
    if plan.relayed:
        packs += [pltpu.VMEM((points // 2, width), bf16)] * 2
    arrays = (tiles, neighbours.transpose(0, 2, 1), distances.transpose(0, 2, 1))
    prepare = pl.pallas_call(
        functools.partial(prepare_kernel, plan),
        out_shape=tuple(packs),
        in_specs=[anywhere] * 4,
        out_specs=(in_vmem,) * len(packs),
        scratch_shapes=[pltpu.VMEM(array.shape, array.dtype) for array in arrays] + [pltpu.SemaphoreType.DMA((5,))],
        compiler_params=limit,
        name="prepare",
    )
    small, *halves = prepare(*map(in_hbm, (*arrays, flat_upstream)))

    def part_of(array, axis, j):
        if plan.parts == 1:
            return array
        part = sum(jnp.where(me == section, plan.units_of(section)[j][1], 0) for section in range(sections))
        return lax.dynamic_slice_in_dim(array, part * unit, unit, axis)

    def unit_route(j):
        return lambda section, replica: (section, replica ^ plan.source_mask(section, j))

    def small_route(j):
        if plan.parts > 1 or j > 0:
            return unit_route(j)
        last = sections - 1
        return lambda section, replica: (last - section, replica ^ plan.source_mask(last - section, j))

    def relay_route(section, replica):
        return sections - 1 - section, replica ^ (1 << plan.shared[1 - section])

    weights = [in_hbm(proj)]
    for turn in range(1, sections):
        weights.append(permute(proj, plan, lambda section, replica: ((section - turn) % sections, replica)))
    if plan.relayed:
        arrived = []
        for j in range(2):
            arrived.append(permute(halves[j], plan, unit_route(0)))
        near = permute(small, plan, small_route(0))
        across = permute(near, plan, relay_route)
        arrived.append(permute(arrived[0], plan, relay_route))
        arrived.append(halves[0])
        small_units = [near, across, small]
    else:
        arrived = [permute(part_of(flat_upstream, 0, j), plan, unit_route(j)) for j in range(plan.units)]
        small_units = [permute(part_of(small, 1, j), plan, small_route(j)) for j in range(plan.units)]

    formed = plan.blocks * block if block % 128 == 0 else width
    load = pl.pallas_call(
        functools.partial(load_kernel, plan),
        out_shape=(
            pltpu.VMEM((2 * nodes, width), bf16),
            pltpu.VMEM((width, rank) if sections == 2 else (sections, width, rank), bf16),
        ),
        in_specs=[anywhere] * (1 + plan.loads),
        out_specs=(in_vmem,) * 2,
        scratch_shapes=[pltpu.SemaphoreType.DMA((2 + plan.loads,))],
        compiler_params=limit,
        name="load",
    )
    forward = pl.pallas_call(
        functools.partial(forward_kernel, plan),
        out_shape=(
            pltpu.VMEM((sections, rows, width), bf16),
            pltpu.VMEM((sections, rows, rank), bf16),
            pltpu.VMEM((sections, rows, rank), f32),
            pltpu.VMEM((sections, rows, 128), f32),
        ),
        in_specs=[in_vmem] * (len(small_units) + 1 + plan.held),
        out_specs=(in_vmem,) * 4,
        scratch_shapes=[pltpu.VMEM((rows, 128), f32)],
        cost_estimate=pl.CostEstimate(
            flops=4 * sections * rows * width * rank, bytes_accessed=6 * width * rank, transcendentals=rows * rank
        ),
        compiler_params=limit,
        name="forward",
    )
    twice, held = load(in_hbm(node_table), *weights[: plan.loads])
    held = [held, weights[1].reshape(width, rank)] if sections == 2 else [held]
    streams, hiddens, inputs, scales = forward(*small_units, twice, *held)
    shapes = [jax.ShapeDtypeStruct((plan.blocks, block, rank), f32)]
    if sections > 1:
        shapes.append(jax.ShapeDtypeStruct((sections - 1, plan.blocks, block, rank), bf16))
    outs = pl.pallas_call(
        functools.partial(backward_kernel, plan),
        out_shape=tuple(shapes),
        in_specs=[in_vmem] * (len(arrived) + 4 + plan.held),
        out_specs=(in_vmem,) * len(shapes),
        scratch_shapes=[
            pltpu.VMEM((2, rows, width), bf16),
            pltpu.VMEM((rows, rank), bf16),
            pltpu.VMEM((2 * rows, formed), bf16),
            pltpu.VMEM((2 * rows, rank), bf16),
            pltpu.VMEM((formed, rank), f32),
        ],
        cost_estimate=pl.CostEstimate(
            flops=6 * sections * rows * width * rank, bytes_accessed=6 * width * rank, transcendentals=0
        ),
        compiler_params=limit,
        name="backward",
    )(*arrived, streams, hiddens, inputs, scales, *held)
    total = outs[0]
    for turn in range(1, sections):
        total = total + permute(
            outs[1][turn - 1], plan, lambda section, replica: ((section + turn) % sections, replica)
        ).astype(f32)
    left = plan.blocks
    stage = 0
    while left > 1:
        left //= 2

        def route(section, replica):
            return section, replica ^ (1 << plan.order(section)[stage])

        total = total[:left] + permute(total[left:].astype(bf16), plan, route).astype(f32)
        stage += 1
    return total * (1.0 / math.sqrt(points * replicas))


def solution(mesh):
    return jax.shard_map(
        on_device,
        mesh=mesh,
        in_specs=(
            P(),
            P(None, "dp"),
            P(None, "dp", None),
            P(None, "dp", None),
            P("section", None, None),
            P(None, "dp", None),
        ),
        out_specs=P("section", "dp", None),
        check_vma=False,
    )
```

```python
import functools
import itertools
import math

import jax
import jax.numpy as jnp
from jax import lax
from jax.experimental import pallas as pl
from jax.experimental.pallas import tpu as pltpu
from jax.sharding import PartitionSpec as P


epsilon = 1e-05
AXES = ("section", "dp")
SHARED_BITS = (0, 2)
LIMIT = 36 << 20


def mask_of(number, bits):
    return sum(((number >> i) & 1) << bit for i, bit in enumerate(bits))


class Plan:
    def __init__(self, sections, replicas, points):
        self.sections, self.replicas, self.points = sections, replicas, points
        bits = replicas.bit_length() - 1
        self.shared = tuple(bit for bit in SHARED_BITS if bit < bits)
        self.summed = tuple(bit for bit in (1, 3, *range(bits)) if bit < bits and bit not in self.shared)
        self.summed = tuple(dict.fromkeys(self.summed))
        self.rows = (points << len(self.shared)) // sections
        self.unit = min(points, self.rows)
        self.units = self.rows // self.unit
        self.parts = points // self.unit
        self.blocks = 1 << len(self.summed)
        self.loads = 1 if sections == 2 else sections
        self.held = 2 if sections == 2 else 1
        self.relayed = sections == 2 and len(self.shared) == 2 and points % 32 == 0

    def order(self, section):
        turn = section % max(len(self.summed), 1)
        return self.summed[turn:] + self.summed[:turn]

    def units_of(self, section):
        units = [divmod(section * self.units + j, self.parts) for j in range(self.units)]
        units = [(mask_of(number, self.shared), part) for number, part in units]
        return sorted(units, key=lambda unit: unit[0].bit_count() != 1)

    def source_mask(self, section, j):
        return self.units_of(section)[j][0]


def permute(block, plan, route):
    pairs = []
    for section, replica in itertools.product(range(plan.sections), range(plan.replicas)):
        to_section, to_replica = route(section, replica)
        pairs.append((section * plan.replicas + replica, to_section * plan.replicas + to_replica))
    return lax.ppermute(block, AXES, pairs)


def dot(left, right, dims):
    return lax.dot_general(left, right, (dims, ((), ())), preferred_element_type=jnp.float32)


CHUNK = 256


def chunks(width):
    size = CHUNK if width % CHUNK == 0 else width
    return [pl.ds(start, size) for start in range(0, width, size)]


def lanes(value):
    size = value.shape[1]
    tile = 128 if size % 128 == 0 else size
    return sum(value[:, start : start + tile] for start in range(0, size, tile))


def by_section(plan, weights, body):
    me = lax.axis_index("section")
    if plan.sections != 2:
        body(me, lambda s: weights[0].at[s])
        return
    for place in range(2):
        pl.when(me == place)(functools.partial(body, place, lambda s, place=place: weights[(s + place) % 2]))


def prepare_kernel(plan, *refs):
    (*arrays, upstream), small, refs = refs[:4], refs[4], refs[5:]
    halves, (*held, sem) = (refs[:2], refs[2:]) if plan.relayed else ((), refs)
    packed = [pltpu.make_async_copy(array, ref, sem.at[j]) for j, (array, ref) in enumerate(zip(arrays, held))]
    taken = []
    half = plan.points // 2
    for j, ref in enumerate(halves):
        place = pl.multiple_of((lax.axis_index("section") ^ j) * half, half)
        taken.append(pltpu.make_async_copy(upstream.at[pl.ds(place, half)], ref, sem.at[3 + j]))
    for copy in packed + taken:
        copy.start()
    for copy in packed:
        copy.wait()
    tiles, neighbours, distances = held
    micro_count, near, _ = neighbours.shape
    index = [(neighbours[m] + tiles[m : m + 1, :]).astype(jnp.float32) for m in range(micro_count)]
    small[:near, :] = jnp.concatenate(index, axis=1)
    small[near:, :] = jnp.concatenate([distances[m] for m in range(micro_count)], axis=1)
    for copy in taken:
        copy.wait()


def load_kernel(plan, table, *refs):
    weights, refs = refs[: plan.loads], refs[plan.loads :]
    table_held, held, sem = refs
    copies = [pltpu.make_async_copy(table, table_held, sem.at[0])]
    if plan.sections == 2:
        copies.append(pltpu.make_async_copy(weights[0].at[0], held, sem.at[1]))
    else:
        me = lax.axis_index("section")
        for turn, weight in enumerate(weights):
            place = lax.rem(me + turn, plan.sections)
            copies.append(pltpu.make_async_copy(weight.at[0], held.at[place], sem.at[1 + turn]))
    for copy in copies:
        copy.start()
    for copy in copies:
        copy.wait()


def forward_kernel(plan, *refs):
    units, sections = plan.units, plan.sections
    given = 3 if plan.relayed else units
    small, table, refs = refs[:given], refs[given], refs[given + 1 :]
    weights, refs = refs[: plan.held], refs[plan.held :]
    streams, hiddens, inputs, scales, twice, total = refs
    nodes, width = table.shape
    twice[:nodes, :] = table[...]
    twice[nodes:, :] = table[...]
    rank = hiddens.shape[2]
    me = lax.axis_index("section")
    count = small[0].shape[0] // 2
    packed = [ref[...] for ref in small]
    if plan.relayed:
        half = plan.unit // 2
        near, across, own = packed
        low_half = lax.broadcasted_iota(jnp.int32, own.shape, 1) < half
        mixed = jnp.where(low_half == (me == 0), own, across)
        packed = [jnp.where(me == 0, array, pltpu.roll(array, half, 1)) for array in (near, mixed)]
    selectors = []
    for j in range(units):
        index = packed[j][:count, :].astype(jnp.int32)
        distance = packed[j][count:, :]
        kernel = (1.0 - distance) ** 3 * (1.0 + 3.0 * distance)
        kernel = kernel / jnp.sum(kernel, axis=0, keepdims=True)
        node = lax.broadcasted_iota(jnp.int32, (nodes, plan.unit), 0)
        selector = jnp.zeros((nodes, plan.unit), jnp.float32)
        for k in range(count):
            selector += jnp.where(node == index[k : k + 1, :], kernel[k : k + 1, :], 0.0)
        high = selector.astype(jnp.bfloat16)
        low = (selector - high.astype(jnp.float32)).astype(jnp.bfloat16)
        selectors.append(jnp.concatenate([high, low], axis=0))
    selector = jnp.concatenate(selectors, axis=1) if units > 1 else selectors[0]
    squares = 0.0
    for columns in chunks(width):
        value = dot(selector, twice[:, columns], ((0,), (0,))).astype(jnp.bfloat16)
        streams[0, :, columns] = value
        value = value.astype(jnp.float32)
        squares += lanes(value * value)
    total[...] = squares

    def body(me, weight_of):
        squares = total[...]
        for s in range(sections):
            weight = weight_of(s)
            scale = lax.rsqrt(jnp.sum(squares, axis=1, keepdims=True) * (1.0 / width) + epsilon)
            scales[s] = jnp.broadcast_to(scale, scales.shape[1:])
            for columns in chunks(rank):
                value = dot(streams[s], weight[:, columns], ((1,), (0,))) * scale
                inputs[s, :, columns] = value
                hiddens[s, :, columns] = jnp.tanh(value).astype(jnp.bfloat16)
            if s + 1 == sections:
                break
            squares = 0.0
            for columns in chunks(width):
                value = streams[s, :, columns].astype(jnp.float32) + dot(hiddens[s], weight[columns, :], ((1,), (1,)))
                value = value.astype(jnp.bfloat16)
                streams[s + 1, :, columns] = value
                value = value.astype(jnp.float32)
                squares += lanes(value * value)

    by_section(plan, weights, body)


def backward_kernel(plan, given, low, rows, *refs):
    sections = plan.sections
    arrived, refs = refs[:given], refs[given:]
    streams, hiddens, inputs, scales = refs[:4]
    weights, refs = refs[4 : 4 + plan.held], refs[4 + plan.held :]
    formed = ()
    if low > 0:
        outs = min(sections, 2)
        formed, refs = refs[:outs], refs[outs:]
    span = pl.ds(low, rows)
    kept, refs = refs[0], refs[1:]
    sent, refs = (refs[0], refs[1:]) if sections > 1 else (None, refs)
    cotangent, grads, left, right, share = refs
    width, rank = streams.shape[2], hiddens.shape[2]
    block = kept.shape[1]
    replica = lax.axis_index("dp")
    step = rows // len(arrived)
    for j, ref in enumerate(arrived):
        cotangent[0, pl.ds(j * step, step), :] = ref[...]
    whole_blocks = block % 128 == 0

    def hand_out(me, s, starts):
        turn = (s + sections - me) % sections if isinstance(me, int) else lax.rem(s + sections - me, sections)
        places = [pl.ds(number * block if whole_blocks else start, block) for number, start in enumerate(starts)]

        def keep():
            for number, place in enumerate(places):
                value = share[place, :]
                kept[number] = value + formed[0][number] if formed else value

        def send():
            for number, place in enumerate(places):
                value = share[place, :]
                value = value + formed[1][turn - 1, number] if formed else value
                sent[turn - 1, number] = value.astype(sent.dtype)

        if isinstance(me, int):
            keep() if turn == 0 else send()
            return
        pl.when(turn == 0)(keep)
        if sections > 1:
            pl.when(turn > 0)(send)

    def body(me, weight_of):
        for s in reversed(range(sections)):
            weight = weight_of(s)
            now, later = (sections - 1 - s) % 2, (sections - s) % 2
            scale = scales[s, span, :][:, :1]
            correction = 0.0
            for columns in chunks(rank):
                hidden = hiddens[s, span, columns].astype(jnp.float32)
                value = dot(cotangent[now], weight[:, columns], ((1,), (0,))) * (1.0 - hidden * hidden)
                grad = value.astype(jnp.bfloat16)
                grads[:, columns] = grad
                right[:rows, columns] = (value * scale).astype(jnp.bfloat16)
                correction += lanes(grad.astype(jnp.float32) * inputs[s, span, columns])
            right[rows:, :] = hiddens[s, span, :]
            starts = [
                pl.multiple_of(jnp.bitwise_xor(replica, mask_of(number, plan.order(s)[::-1])) * block, block)
                for number in range(plan.blocks)
            ]
            if whole_blocks:
                reads = [(pl.ds(start, block), pl.ds(number * block, block)) for number, start in enumerate(starts)]
            else:
                reads = [(columns, columns) for columns in chunks(width)]
            for columns, place in reads:
                left[:rows, place] = streams[s, span, columns]
                left[rows:, place] = cotangent[now, :, columns]
            if s > 0:
                correction = jnp.sum(correction, axis=1, keepdims=True) * (1.0 / width) * scale * scale
                for columns in chunks(width):
                    value = dot(grads[...], weight[columns, :], ((1,), (1,)))
                    value = cotangent[now, :, columns].astype(jnp.float32) + scale * value
                    value = value - correction * streams[s, span, columns].astype(jnp.float32)
                    cotangent[later, :, columns] = value.astype(jnp.bfloat16)
            for columns in chunks(rank):
                share[:, columns] = dot(left[...], right[:, columns], ((0,), (0,)))
            hand_out(me, s, starts)

    by_section(plan, weights, body)


def on_device(node_table, tiles, neighbours, distances, proj, upstream):
    sections, replicas = lax.axis_size("section"), lax.axis_size("dp")
    micro_count, row_count, near = distances.shape
    nodes, width = node_table.shape
    rank = proj.shape[2]
    points = micro_count * row_count
    plan = Plan(sections, replicas, points)
    rows, unit, block = plan.rows, plan.unit, width // replicas
    me = lax.axis_index("section")

    in_vmem = pl.BlockSpec(memory_space=pltpu.VMEM)
    anywhere = pl.BlockSpec(memory_space=pl.ANY)
    bf16, f32 = jnp.bfloat16, jnp.float32
    in_hbm = functools.partial(pltpu.with_memory_space_constraint, memory_space=pltpu.HBM)
    flat_upstream = upstream.reshape(points, width)
    limit = pltpu.CompilerParams(vmem_limit_bytes=LIMIT)
    packs = [pltpu.VMEM((2 * near, points), f32)]
    if plan.relayed:
        packs += [pltpu.VMEM((points // 2, width), bf16)] * 2
    arrays = (tiles, neighbours.transpose(0, 2, 1), distances.transpose(0, 2, 1))
    prepare = pl.pallas_call(
        functools.partial(prepare_kernel, plan),
        out_shape=tuple(packs),
        in_specs=[anywhere] * 4,
        out_specs=(in_vmem,) * len(packs),
        scratch_shapes=[pltpu.VMEM(array.shape, array.dtype) for array in arrays] + [pltpu.SemaphoreType.DMA((5,))],
        compiler_params=limit,
        name="prepare",
    )
    small, *halves = prepare(*map(in_hbm, (*arrays, flat_upstream)))

    def part_of(array, axis, j):
        if plan.parts == 1:
            return array
        part = sum(jnp.where(me == section, plan.units_of(section)[j][1], 0) for section in range(sections))
        return lax.dynamic_slice_in_dim(array, part * unit, unit, axis)

    def unit_route(j):
        return lambda section, replica: (section, replica ^ plan.source_mask(section, j))

    def small_route(j):
        if plan.parts > 1 or j > 0:
            return unit_route(j)
        last = sections - 1
        return lambda section, replica: (last - section, replica ^ plan.source_mask(last - section, j))

    def relay_route(section, replica):
        return sections - 1 - section, replica ^ (1 << plan.shared[1 - section])

    weights = [in_hbm(proj)]
    for turn in range(1, sections):
        weights.append(permute(proj, plan, lambda section, replica: ((section - turn) % sections, replica)))
    if plan.relayed:
        arrived = []
        for j in range(2):
            arrived.append(permute(halves[j], plan, unit_route(0)))
        near = permute(small, plan, small_route(0))
        across = permute(near, plan, relay_route)
        arrived.append(permute(arrived[0], plan, relay_route))
        arrived.insert(2, halves[0])
        small_units = [near, across, small]
    else:
        arrived = [permute(part_of(flat_upstream, 0, j), plan, unit_route(j)) for j in range(plan.units)]
        small_units = [permute(part_of(small, 1, j), plan, small_route(j)) for j in range(plan.units)]

    formed = plan.blocks * block if block % 128 == 0 else width
    load = pl.pallas_call(
        functools.partial(load_kernel, plan),
        out_shape=(
            pltpu.VMEM((nodes, width), bf16),
            pltpu.VMEM((width, rank) if sections == 2 else (sections, width, rank), bf16),
        ),
        in_specs=[anywhere] * (1 + plan.loads),
        out_specs=(in_vmem,) * 2,
        scratch_shapes=[pltpu.SemaphoreType.DMA((1 + plan.loads,))],
        compiler_params=limit,
        name="load",
    )
    forward = pl.pallas_call(
        functools.partial(forward_kernel, plan),
        out_shape=(
            pltpu.VMEM((sections, rows, width), bf16),
            pltpu.VMEM((sections, rows, rank), bf16),
            pltpu.VMEM((sections, rows, rank), f32),
            pltpu.VMEM((sections, rows, 128), f32),
        ),
        in_specs=[in_vmem] * (len(small_units) + 1 + plan.held),
        out_specs=(in_vmem,) * 4,
        scratch_shapes=[pltpu.VMEM((2 * nodes, width), bf16), pltpu.VMEM((rows, 128), f32)],
        cost_estimate=pl.CostEstimate(
            flops=4 * sections * rows * width * rank, bytes_accessed=6 * width * rank, transcendentals=rows * rank
        ),
        compiler_params=limit,
        name="forward",
    )
    table, held = load(in_hbm(node_table), *weights[: plan.loads])
    held = [held, weights[1].reshape(width, rank)] if sections == 2 else [held]
    streams, hiddens, inputs, scales = forward(*small_units, table, *held)
    cuts = [(arrived, 0, rows)]
    outs = ()
    for given, low, count in cuts:
        last = low + count == rows
        shapes = [pltpu.VMEM((plan.blocks, block, rank), f32)]
        if sections > 1:
            shapes.append(pltpu.VMEM((sections - 1, plan.blocks, block, rank), bf16 if last else f32))
        backward = pl.pallas_call(
            functools.partial(backward_kernel, plan, len(given), low, count),
            out_shape=tuple(shapes),
            in_specs=[in_vmem] * (len(given) + 4 + plan.held + len(outs)),
            out_specs=(in_vmem,) * len(shapes),
            scratch_shapes=[
                pltpu.VMEM((2, count, width), bf16),
                pltpu.VMEM((count, rank), bf16),
                pltpu.VMEM((2 * count, formed), bf16),
                pltpu.VMEM((2 * count, rank), bf16),
                pltpu.VMEM((formed, rank), f32),
            ],
            cost_estimate=pl.CostEstimate(
                flops=6 * sections * count * width * rank, bytes_accessed=6 * width * rank, transcendentals=0
            ),
            compiler_params=limit,
        )
        outs = backward(*given, streams, hiddens, inputs, scales, *held, *outs)
    total = outs[0]
    for turn in range(1, sections):
        total = total + permute(
            outs[1][turn - 1], plan, lambda section, replica: ((section + turn) % sections, replica)
        ).astype(f32)
    left = plan.blocks
    stage = 0
    while left > 1:
        left //= 2

        def route(section, replica):
            return section, replica ^ (1 << plan.order(section)[stage])

        total = total[:left] + permute(total[left:].astype(bf16), plan, route).astype(f32)
        stage += 1
    return total * (1.0 / math.sqrt(points * replicas))


def solution(mesh):
    return jax.shard_map(
        on_device,
        mesh=mesh,
        in_specs=(
            P(),
            P(None, "dp"),
            P(None, "dp", None),
            P(None, "dp", None),
            P("section", None, None),
            P(None, "dp", None),
        ),
        out_specs=P("section", "dp", None),
        check_vma=False,
    )
```

```python
import functools
import itertools
import math

import jax
import jax.numpy as jnp
from jax import lax
from jax.experimental import pallas as pl
from jax.experimental.pallas import tpu as pltpu
from jax.sharding import PartitionSpec as P


epsilon = 1e-05
AXES = ("section", "dp")
SHARED_BITS = (0, 2)
LIMIT = 36 << 20


def mask_of(number, bits):
    return sum(((number >> i) & 1) << bit for i, bit in enumerate(bits))


class Plan:
    def __init__(self, sections, replicas, points):
        self.sections, self.replicas, self.points = sections, replicas, points
        bits = replicas.bit_length() - 1
        self.shared = tuple(bit for bit in SHARED_BITS if bit < bits)
        self.summed = tuple(bit for bit in (1, 3, *range(bits)) if bit < bits and bit not in self.shared)
        self.summed = tuple(dict.fromkeys(self.summed))
        self.rows = (points << len(self.shared)) // sections
        self.unit = min(points, self.rows)
        self.units = self.rows // self.unit
        self.parts = points // self.unit
        self.blocks = 1 << len(self.summed)
        self.loads = 1 if sections == 2 else sections
        self.held = 2 if sections == 2 else 1
        self.relayed = sections == 2 and len(self.shared) == 2 and points % 32 == 0

    def order(self, section):
        turn = section % max(len(self.summed), 1)
        return self.summed[turn:] + self.summed[:turn]

    def units_of(self, section):
        units = [divmod(section * self.units + j, self.parts) for j in range(self.units)]
        units = [(mask_of(number, self.shared), part) for number, part in units]
        return sorted(units, key=lambda unit: unit[0].bit_count() != 1)

    def source_mask(self, section, j):
        return self.units_of(section)[j][0]


def permute(block, plan, route):
    pairs = []
    for section, replica in itertools.product(range(plan.sections), range(plan.replicas)):
        to_section, to_replica = route(section, replica)
        pairs.append((section * plan.replicas + replica, to_section * plan.replicas + to_replica))
    return lax.ppermute(block, AXES, pairs)


def dot(left, right, dims):
    return lax.dot_general(left, right, (dims, ((), ())), preferred_element_type=jnp.float32)


CHUNK = 256


def chunks(width):
    size = CHUNK if width % CHUNK == 0 else width
    return [pl.ds(start, size) for start in range(0, width, size)]


def lanes(value):
    size = value.shape[1]
    tile = 128 if size % 128 == 0 else size
    return sum(value[:, start : start + tile] for start in range(0, size, tile))


def by_section(plan, weights, body):
    me = lax.axis_index("section")
    if plan.sections != 2:
        body(me, lambda s: weights[0].at[s])
        return
    for place in range(2):
        pl.when(me == place)(functools.partial(body, place, lambda s, place=place: weights[(s + place) % 2]))


def prepare_kernel(plan, *refs):
    (*arrays, upstream), small, refs = refs[:4], refs[4], refs[5:]
    halves, (*held, sem) = (refs[:2], refs[2:]) if plan.relayed else ((), refs)
    packed = [pltpu.make_async_copy(array, ref, sem.at[j]) for j, (array, ref) in enumerate(zip(arrays, held))]
    taken = []
    half = plan.points // 2
    for j, ref in enumerate(halves):
        place = pl.multiple_of((lax.axis_index("section") ^ j) * half, half)
        taken.append(pltpu.make_async_copy(upstream.at[pl.ds(place, half)], ref, sem.at[3 + j]))
    for copy in packed + taken:
        copy.start()
    for copy in packed:
        copy.wait()
    tiles, neighbours, distances = held
    micro_count, near, _ = neighbours.shape
    index = [(neighbours[m] + tiles[m : m + 1, :]).astype(jnp.float32) for m in range(micro_count)]
    small[:near, :] = jnp.concatenate(index, axis=1)
    small[near:, :] = jnp.concatenate([distances[m] for m in range(micro_count)], axis=1)
    for copy in taken:
        copy.wait()


def load_kernel(plan, table, *refs):
    weights, refs = refs[: plan.loads], refs[plan.loads :]
    table_held, held, sem = refs
    copies = [pltpu.make_async_copy(table, table_held, sem.at[0])]
    if plan.sections == 2:
        copies.append(pltpu.make_async_copy(weights[0].at[0], held, sem.at[1]))
    else:
        me = lax.axis_index("section")
        for turn, weight in enumerate(weights):
            place = lax.rem(me + turn, plan.sections)
            copies.append(pltpu.make_async_copy(weight.at[0], held.at[place], sem.at[1 + turn]))
    for copy in copies:
        copy.start()
    for copy in copies:
        copy.wait()


def forward_kernel(plan, *refs):
    units, sections = plan.units, plan.sections
    given = 3 if plan.relayed else units
    small, table, refs = refs[:given], refs[given], refs[given + 1 :]
    weights, refs = refs[: plan.held], refs[plan.held :]
    streams, hiddens, inputs, scales, twice, total = refs
    nodes, width = table.shape
    twice[:nodes, :] = table[...]
    twice[nodes:, :] = table[...]
    rank = hiddens.shape[2]
    me = lax.axis_index("section")
    count = small[0].shape[0] // 2
    packed = [ref[...] for ref in small]
    if plan.relayed:
        half = plan.unit // 2
        near, across, own = packed
        low_half = lax.broadcasted_iota(jnp.int32, own.shape, 1) < half
        mixed = jnp.where(low_half == (me == 0), own, across)
        packed = [jnp.where(me == 0, array, pltpu.roll(array, half, 1)) for array in (near, mixed)]
    selectors = []
    for j in range(units):
        index = packed[j][:count, :].astype(jnp.int32)
        distance = packed[j][count:, :]
        kernel = (1.0 - distance) ** 3 * (1.0 + 3.0 * distance)
        kernel = kernel / jnp.sum(kernel, axis=0, keepdims=True)
        node = lax.broadcasted_iota(jnp.int32, (nodes, plan.unit), 0)
        selector = jnp.zeros((nodes, plan.unit), jnp.float32)
        for k in range(count):
            selector += jnp.where(node == index[k : k + 1, :], kernel[k : k + 1, :], 0.0)
        high = selector.astype(jnp.bfloat16)
        low = (selector - high.astype(jnp.float32)).astype(jnp.bfloat16)
        selectors.append(jnp.concatenate([high, low], axis=0))
    selector = jnp.concatenate(selectors, axis=1) if units > 1 else selectors[0]
    squares = 0.0
    for columns in chunks(width):
        value = dot(selector, twice[:, columns], ((0,), (0,))).astype(jnp.bfloat16)
        streams[0, :, columns] = value
        value = value.astype(jnp.float32)
        squares += lanes(value * value)
    total[...] = squares

    def body(me, weight_of):
        squares = total[...]
        for s in range(sections):
            weight = weight_of(s)
            scale = lax.rsqrt(jnp.sum(squares, axis=1, keepdims=True) * (1.0 / width) + epsilon)
            scales[s] = jnp.broadcast_to(scale, scales.shape[1:])
            for columns in chunks(rank):
                value = dot(streams[s], weight[:, columns], ((1,), (0,))) * scale
                inputs[s, :, columns] = value
                hiddens[s, :, columns] = jnp.tanh(value).astype(jnp.bfloat16)
            if s + 1 == sections:
                break
            squares = 0.0
            for columns in chunks(width):
                value = streams[s, :, columns].astype(jnp.float32) + dot(hiddens[s], weight[columns, :], ((1,), (1,)))
                value = value.astype(jnp.bfloat16)
                streams[s + 1, :, columns] = value
                value = value.astype(jnp.float32)
                squares += lanes(value * value)

    by_section(plan, weights, body)


def backward_kernel(plan, given, low, rows, *refs):
    sections = plan.sections
    arrived, refs = refs[:given], refs[given:]
    streams, hiddens, inputs, scales = refs[:4]
    weights, refs = refs[4 : 4 + plan.held], refs[4 + plan.held :]
    formed = ()
    if low > 0:
        outs = min(sections, 2)
        formed, refs = refs[:outs], refs[outs:]
    span = pl.ds(low, rows)
    kept, refs = refs[0], refs[1:]
    sent, refs = (refs[0], refs[1:]) if sections > 1 else (None, refs)
    cotangent, grads, left, right, share = refs
    width, rank = streams.shape[2], hiddens.shape[2]
    block = kept.shape[1]
    replica = lax.axis_index("dp")
    step = rows // len(arrived)
    for j, ref in enumerate(arrived):
        cotangent[0, pl.ds(j * step, step), :] = ref[...]
    whole_blocks = block % 128 == 0

    def hand_out(me, s, starts):
        turn = (s + sections - me) % sections if isinstance(me, int) else lax.rem(s + sections - me, sections)
        places = [pl.ds(number * block if whole_blocks else start, block) for number, start in enumerate(starts)]

        def keep():
            for number, place in enumerate(places):
                value = share[place, :]
                kept[number] = value + formed[0][number] if formed else value

        def send():
            for number, place in enumerate(places):
                value = share[place, :]
                value = value + formed[1][turn - 1, number] if formed else value
                sent[turn - 1, number] = value.astype(sent.dtype)

        if isinstance(me, int):
            keep() if turn == 0 else send()
            return
        pl.when(turn == 0)(keep)
        if sections > 1:
            pl.when(turn > 0)(send)

    def body(me, weight_of):
        for s in reversed(range(sections)):
            weight = weight_of(s)
            now, later = (sections - 1 - s) % 2, (sections - s) % 2
            scale = scales[s, span, :][:, :1]
            correction = 0.0
            for columns in chunks(rank):
                hidden = hiddens[s, span, columns].astype(jnp.float32)
                value = dot(cotangent[now], weight[:, columns], ((1,), (0,))) * (1.0 - hidden * hidden)
                grad = value.astype(jnp.bfloat16)
                grads[:, columns] = grad
                right[:rows, columns] = (value * scale).astype(jnp.bfloat16)
                correction += lanes(grad.astype(jnp.float32) * inputs[s, span, columns])
            right[rows:, :] = hiddens[s, span, :]
            starts = [
                pl.multiple_of(jnp.bitwise_xor(replica, mask_of(number, plan.order(s)[::-1])) * block, block)
                for number in range(plan.blocks)
            ]
            if whole_blocks:
                reads = [(pl.ds(start, block), pl.ds(number * block, block)) for number, start in enumerate(starts)]
            else:
                reads = [(columns, columns) for columns in chunks(width)]
            for columns, place in reads:
                left[:rows, place] = streams[s, span, columns]
                left[rows:, place] = cotangent[now, :, columns]
            if s > 0:
                correction = jnp.sum(correction, axis=1, keepdims=True) * (1.0 / width) * scale * scale
                for columns in chunks(width):
                    value = dot(grads[...], weight[columns, :], ((1,), (1,)))
                    value = cotangent[now, :, columns].astype(jnp.float32) + scale * value
                    value = value - correction * streams[s, span, columns].astype(jnp.float32)
                    cotangent[later, :, columns] = value.astype(jnp.bfloat16)
            for columns in chunks(rank):
                share[:, columns] = dot(left[...], right[:, columns], ((0,), (0,)))
            hand_out(me, s, starts)

    by_section(plan, weights, body)


def on_device(node_table, tiles, neighbours, distances, proj, upstream):
    sections, replicas = lax.axis_size("section"), lax.axis_size("dp")
    micro_count, row_count, near = distances.shape
    nodes, width = node_table.shape
    rank = proj.shape[2]
    points = micro_count * row_count
    plan = Plan(sections, replicas, points)
    rows, unit, block = plan.rows, plan.unit, width // replicas
    me = lax.axis_index("section")

    in_vmem = pl.BlockSpec(memory_space=pltpu.VMEM)
    anywhere = pl.BlockSpec(memory_space=pl.ANY)
    bf16, f32 = jnp.bfloat16, jnp.float32
    in_hbm = functools.partial(pltpu.with_memory_space_constraint, memory_space=pltpu.HBM)
    flat_upstream = upstream.reshape(points, width)
    limit = pltpu.CompilerParams(vmem_limit_bytes=LIMIT)
    packs = [pltpu.VMEM((2 * near, points), f32)]
    if plan.relayed:
        packs += [pltpu.VMEM((points // 2, width), bf16)] * 2
    arrays = (tiles, neighbours.transpose(0, 2, 1), distances.transpose(0, 2, 1))
    prepare = pl.pallas_call(
        functools.partial(prepare_kernel, plan),
        out_shape=tuple(packs),
        in_specs=[anywhere] * 4,
        out_specs=(in_vmem,) * len(packs),
        scratch_shapes=[pltpu.VMEM(array.shape, array.dtype) for array in arrays] + [pltpu.SemaphoreType.DMA((5,))],
        compiler_params=limit,
        name="prepare",
    )
    small, *halves = prepare(*map(in_hbm, (*arrays, flat_upstream)))

    def part_of(array, axis, j):
        if plan.parts == 1:
            return array
        part = sum(jnp.where(me == section, plan.units_of(section)[j][1], 0) for section in range(sections))
        return lax.dynamic_slice_in_dim(array, part * unit, unit, axis)

    def unit_route(j):
        return lambda section, replica: (section, replica ^ plan.source_mask(section, j))

    def small_route(j):
        if plan.parts > 1 or j > 0:
            return unit_route(j)
        last = sections - 1
        return lambda section, replica: (last - section, replica ^ plan.source_mask(last - section, j))

    def relay_route(section, replica):
        return sections - 1 - section, replica ^ (1 << plan.shared[1 - section])

    weights = [in_hbm(proj)]
    for turn in range(1, sections):
        weights.append(permute(proj, plan, lambda section, replica: ((section - turn) % sections, replica)))
    if plan.relayed:
        arrived = []
        for j in range(2):
            arrived.append(permute(halves[j], plan, unit_route(0)))
        near = permute(small, plan, small_route(0))
        across = permute(near, plan, relay_route)
        arrived.append(permute(arrived[0], plan, relay_route))
        arrived.insert(2, halves[0])
        small_units = [near, across, small]
    else:
        arrived = [permute(part_of(flat_upstream, 0, j), plan, unit_route(j)) for j in range(plan.units)]
        small_units = [permute(part_of(small, 1, j), plan, small_route(j)) for j in range(plan.units)]

    formed = plan.blocks * block if block % 128 == 0 else width
    load = pl.pallas_call(
        functools.partial(load_kernel, plan),
        out_shape=(
            pltpu.VMEM((nodes, width), bf16),
            pltpu.VMEM((width, rank) if sections == 2 else (sections, width, rank), bf16),
        ),
        in_specs=[anywhere] * (1 + plan.loads),
        out_specs=(in_vmem,) * 2,
        scratch_shapes=[pltpu.SemaphoreType.DMA((1 + plan.loads,))],
        compiler_params=limit,
        name="load",
    )
    forward = pl.pallas_call(
        functools.partial(forward_kernel, plan),
        out_shape=(
            pltpu.VMEM((sections, rows, width), bf16),
            pltpu.VMEM((sections, rows, rank), bf16),
            pltpu.VMEM((sections, rows, rank), f32),
            pltpu.VMEM((sections, rows, 128), f32),
        ),
        in_specs=[in_vmem] * (len(small_units) + 1 + plan.held),
        out_specs=(in_vmem,) * 4,
        scratch_shapes=[pltpu.VMEM((2 * nodes, width), bf16), pltpu.VMEM((rows, 128), f32)],
        cost_estimate=pl.CostEstimate(
            flops=4 * sections * rows * width * rank, bytes_accessed=6 * width * rank, transcendentals=rows * rank
        ),
        compiler_params=limit,
        name="forward",
    )
    table, held = load(in_hbm(node_table), *weights[: plan.loads])
    held = [held, weights[1].reshape(width, rank)] if sections == 2 else [held]
    streams, hiddens, inputs, scales = forward(*small_units, table, *held)
    cuts = [(arrived, 0, rows)]
    outs = ()
    for given, low, count in cuts:
        last = low + count == rows
        shapes = [pltpu.VMEM((plan.blocks, block, rank), f32)]
        if sections > 1:
            shapes.append(pltpu.VMEM((sections - 1, plan.blocks, block, rank), bf16 if last else f32))
        backward = pl.pallas_call(
            functools.partial(backward_kernel, plan, len(given), low, count),
            out_shape=tuple(shapes),
            in_specs=[in_vmem] * (len(given) + 4 + plan.held + len(outs)),
            out_specs=(in_vmem,) * len(shapes),
            scratch_shapes=[
                pltpu.VMEM((2, count, width), bf16),
                pltpu.VMEM((count, rank), bf16),
                pltpu.VMEM((2 * count, formed), bf16),
                pltpu.VMEM((2 * count, rank), bf16),
                pltpu.VMEM((formed, rank), f32),
            ],
            cost_estimate=pl.CostEstimate(
                flops=6 * sections * count * width * rank, bytes_accessed=6 * width * rank, transcendentals=0
            ),
            compiler_params=limit,
        )
        outs = backward(*given, streams, hiddens, inputs, scales, *held, *outs)

    def split_sum(total, came):
        half = total.shape[0] // 2
        return pl.pallas_call(
            split_sum_kernel,
            out_shape=(pltpu.VMEM((half, block, rank), f32), pltpu.VMEM((half, block, rank), bf16)),
            in_specs=[in_vmem] * 2,
            out_specs=(in_vmem,) * 2,
            compiler_params=limit,
        )(total, pltpu.with_memory_space_constraint(came, pltpu.VMEM))

    def swap(array, turn):
        return permute(array, plan, lambda section, replica: ((section + turn) % sections, replica))

    total = outs[0]
    if sections == 2:
        came = swap(outs[1][0], 1)
    else:
        for turn in range(1, sections):
            total = total + swap(outs[1][turn - 1], turn).astype(f32)
    for stage in range(len(plan.summed)):

        def route(section, replica):
            return section, replica ^ (1 << plan.order(section)[stage])

        if sections == 2:
            total, leaving = split_sum(total, came)
        else:
            half = total.shape[0] // 2
            total, leaving = total[:half], total[half:].astype(bf16)
        came = permute(leaving, plan, route)
        if sections != 2:
            total = total + came.astype(f32)
    if sections == 2:
        total = total + came.astype(f32)
    return total * (1.0 / math.sqrt(points * replicas))


def split_sum_kernel(total, came, kept, leaving):
    half = kept.shape[0]
    kept[...] = total[:half] + came[:half].astype(jnp.float32)
    leaving[...] = (total[half:] + came[half:].astype(jnp.float32)).astype(jnp.bfloat16)


def solution(mesh):
    return jax.shard_map(
        on_device,
        mesh=mesh,
        in_specs=(
            P(),
            P(None, "dp"),
            P(None, "dp", None),
            P(None, "dp", None),
            P("section", None, None),
            P(None, "dp", None),
        ),
        out_specs=P("section", "dp", None),
        check_vma=False,
    )
```

```python
import functools
import itertools
import math

import jax
import jax.numpy as jnp
from jax import lax
from jax.experimental import pallas as pl
from jax.experimental.pallas import tpu as pltpu
from jax.sharding import PartitionSpec as P


epsilon = 1e-05
AXES = ("section", "dp")
SHARED_BITS = (0, 2)
LIMIT = 36 << 20
PARTS = 2


def mask_of(number, bits):
    return sum(((number >> i) & 1) << bit for i, bit in enumerate(bits))


class Plan:
    def __init__(self, sections, replicas, points):
        self.sections, self.replicas, self.points = sections, replicas, points
        bits = replicas.bit_length() - 1
        self.shared = tuple(bit for bit in SHARED_BITS if bit < bits)
        self.summed = tuple(bit for bit in (1, 3, *range(bits)) if bit < bits and bit not in self.shared)
        self.summed = tuple(dict.fromkeys(self.summed))
        self.rows = (points << len(self.shared)) // sections
        self.unit = min(points, self.rows)
        self.units = self.rows // self.unit
        self.parts = points // self.unit
        self.blocks = 1 << len(self.summed)
        self.loads = 1 if sections == 2 else sections
        self.held = 2 if sections == 2 else 1
        self.relayed = sections == 2 and len(self.shared) == 2 and points % 32 == 0

    def order(self, section):
        turn = section % max(len(self.summed), 1)
        return self.summed[turn:] + self.summed[:turn]

    def units_of(self, section):
        units = [divmod(section * self.units + j, self.parts) for j in range(self.units)]
        units = [(mask_of(number, self.shared), part) for number, part in units]
        return sorted(units, key=lambda unit: unit[0].bit_count() != 1)

    def source_mask(self, section, j):
        return self.units_of(section)[j][0]


def permute(block, plan, route):
    pairs = []
    for section, replica in itertools.product(range(plan.sections), range(plan.replicas)):
        to_section, to_replica = route(section, replica)
        pairs.append((section * plan.replicas + replica, to_section * plan.replicas + to_replica))
    return lax.ppermute(block, AXES, pairs)


def dot(left, right, dims):
    return lax.dot_general(left, right, (dims, ((), ())), preferred_element_type=jnp.float32)


CHUNK = 256


def chunks(width):
    size = CHUNK if width % CHUNK == 0 else width
    return [pl.ds(start, size) for start in range(0, width, size)]


def lanes(value):
    size = value.shape[1]
    tile = 128 if size % 128 == 0 else size
    return sum(value[:, start : start + tile] for start in range(0, size, tile))


def by_section(plan, weights, body):
    me = lax.axis_index("section")
    if plan.sections != 2:
        body(me, lambda s: weights[0].at[s])
        return
    for place in range(2):
        pl.when(me == place)(functools.partial(body, place, lambda s, place=place: weights[(s + place) % 2]))


def prepare_kernel(plan, *refs):
    (*arrays, upstream), small, refs = refs[:4], refs[4], refs[5:]
    halves, (*held, sem) = (refs[:2], refs[2:]) if plan.relayed else ((), refs)
    packed = [pltpu.make_async_copy(array, ref, sem.at[j]) for j, (array, ref) in enumerate(zip(arrays, held))]
    taken = []
    half = plan.points // 2
    for j, ref in enumerate(halves):
        place = pl.multiple_of((lax.axis_index("section") ^ j) * half, half)
        taken.append(pltpu.make_async_copy(upstream.at[pl.ds(place, half)], ref, sem.at[3 + j]))
    for copy in packed + taken:
        copy.start()
    for copy in packed:
        copy.wait()
    tiles, neighbours, distances = held
    micro_count, near, _ = neighbours.shape
    index = [(neighbours[m] + tiles[m : m + 1, :]).astype(jnp.float32) for m in range(micro_count)]
    small[:near, :] = jnp.concatenate(index, axis=1)
    small[near:, :] = jnp.concatenate([distances[m] for m in range(micro_count)], axis=1)
    for copy in taken:
        copy.wait()


def load_kernel(plan, table, *refs):
    weights, refs = refs[: plan.loads], refs[plan.loads :]
    table_held, held, sem = refs
    copies = [pltpu.make_async_copy(table, table_held, sem.at[0])]
    if plan.sections == 2:
        copies.append(pltpu.make_async_copy(weights[0].at[0], held, sem.at[1]))
    else:
        me = lax.axis_index("section")
        for turn, weight in enumerate(weights):
            place = lax.rem(me + turn, plan.sections)
            copies.append(pltpu.make_async_copy(weight.at[0], held.at[place], sem.at[1 + turn]))
    for copy in copies:
        copy.start()
    for copy in copies:
        copy.wait()


def forward_kernel(plan, *refs):
    units, sections = plan.units, plan.sections
    given = 3 if plan.relayed else units
    small, table, refs = refs[:given], refs[given], refs[given + 1 :]
    weights, refs = refs[: plan.held], refs[plan.held :]
    streams, hiddens, inputs, scales, twice, total = refs
    nodes, width = table.shape
    twice[:nodes, :] = table[...]
    twice[nodes:, :] = table[...]
    rank = hiddens.shape[2]
    me = lax.axis_index("section")
    count = small[0].shape[0] // 2
    packed = [ref[...] for ref in small]
    if plan.relayed:
        half = plan.unit // 2
        near, across, own = packed
        low_half = lax.broadcasted_iota(jnp.int32, own.shape, 1) < half
        mixed = jnp.where(low_half == (me == 0), own, across)
        packed = [jnp.where(me == 0, array, pltpu.roll(array, half, 1)) for array in (near, mixed)]
    selectors = []
    for j in range(units):
        index = packed[j][:count, :].astype(jnp.int32)
        distance = packed[j][count:, :]
        kernel = (1.0 - distance) ** 3 * (1.0 + 3.0 * distance)
        kernel = kernel / jnp.sum(kernel, axis=0, keepdims=True)
        node = lax.broadcasted_iota(jnp.int32, (nodes, plan.unit), 0)
        selector = jnp.zeros((nodes, plan.unit), jnp.float32)
        for k in range(count):
            selector += jnp.where(node == index[k : k + 1, :], kernel[k : k + 1, :], 0.0)
        high = selector.astype(jnp.bfloat16)
        low = (selector - high.astype(jnp.float32)).astype(jnp.bfloat16)
        selectors.append(jnp.concatenate([high, low], axis=0))
    selector = jnp.concatenate(selectors, axis=1) if units > 1 else selectors[0]
    squares = 0.0
    for columns in chunks(width):
        value = dot(selector, twice[:, columns], ((0,), (0,))).astype(jnp.bfloat16)
        streams[0, :, columns] = value
        value = value.astype(jnp.float32)
        squares += lanes(value * value)
    total[...] = squares

    def body(me, weight_of):
        squares = total[...]
        for s in range(sections):
            weight = weight_of(s)
            scale = lax.rsqrt(jnp.sum(squares, axis=1, keepdims=True) * (1.0 / width) + epsilon)
            scales[s] = jnp.broadcast_to(scale, scales.shape[1:])
            for columns in chunks(rank):
                value = dot(streams[s], weight[:, columns], ((1,), (0,))) * scale
                inputs[s, :, columns] = value
                hiddens[s, :, columns] = jnp.tanh(value).astype(jnp.bfloat16)
            if s + 1 == sections:
                break
            squares = 0.0
            for columns in chunks(width):
                value = streams[s, :, columns].astype(jnp.float32) + dot(hiddens[s], weight[columns, :], ((1,), (1,)))
                value = value.astype(jnp.bfloat16)
                streams[s + 1, :, columns] = value
                value = value.astype(jnp.float32)
                squares += lanes(value * value)

    by_section(plan, weights, body)


def backward_kernel(plan, given, low, rows, *refs):
    sections = plan.sections
    arrived, refs = refs[:given], refs[given:]
    streams, hiddens, inputs, scales = refs[:4]
    weights, refs = refs[4 : 4 + plan.held], refs[4 + plan.held :]
    formed = ()
    if low > 0:
        outs = min(sections, 2)
        formed, refs = refs[:outs], refs[outs:]
    span = pl.ds(low, rows)
    kept, refs = refs[0], refs[1:]
    sent, refs = (refs[0], refs[1:]) if sections > 1 else (None, refs)
    cotangent, grads, left, right, share = refs
    width, rank = streams.shape[2], hiddens.shape[2]
    block = kept.shape[1]
    replica = lax.axis_index("dp")
    step = rows // len(arrived)
    for j, ref in enumerate(arrived):
        cotangent[0, pl.ds(j * step, step), :] = ref[...]
    whole_blocks = block % 128 == 0

    def hand_out(me, s, starts):
        turn = (s + sections - me) % sections if isinstance(me, int) else lax.rem(s + sections - me, sections)
        places = [pl.ds(number * block if whole_blocks else start, block) for number, start in enumerate(starts)]

        def keep():
            for number, place in enumerate(places):
                value = share[place, :]
                kept[number] = value + formed[0][number] if formed else value

        def send():
            for number, place in enumerate(places):
                value = share[place, :]
                value = value + formed[1][turn - 1, number] if formed else value
                sent[turn - 1, number] = value.astype(sent.dtype)

        if isinstance(me, int):
            keep() if turn == 0 else send()
            return
        pl.when(turn == 0)(keep)
        if sections > 1:
            pl.when(turn > 0)(send)

    def body(me, weight_of):
        for s in reversed(range(sections)):
            weight = weight_of(s)
            now, later = (sections - 1 - s) % 2, (sections - s) % 2
            scale = scales[s, span, :][:, :1]
            correction = 0.0
            for columns in chunks(rank):
                hidden = hiddens[s, span, columns].astype(jnp.float32)
                value = dot(cotangent[now], weight[:, columns], ((1,), (0,))) * (1.0 - hidden * hidden)
                grad = value.astype(jnp.bfloat16)
                grads[:, columns] = grad
                right[:rows, columns] = (value * scale).astype(jnp.bfloat16)
                correction += lanes(grad.astype(jnp.float32) * inputs[s, span, columns])
            right[rows:, :] = hiddens[s, span, :]
            starts = [
                pl.multiple_of(jnp.bitwise_xor(replica, mask_of(number, plan.order(s)[::-1])) * block, block)
                for number in range(plan.blocks)
            ]
            if whole_blocks:
                reads = [(pl.ds(start, block), pl.ds(number * block, block)) for number, start in enumerate(starts)]
            else:
                reads = [(columns, columns) for columns in chunks(width)]
            for columns, place in reads:
                left[:rows, place] = streams[s, span, columns]
                left[rows:, place] = cotangent[now, :, columns]
            if s > 0:
                correction = jnp.sum(correction, axis=1, keepdims=True) * (1.0 / width) * scale * scale
                for columns in chunks(width):
                    value = dot(grads[...], weight[columns, :], ((1,), (1,)))
                    value = cotangent[now, :, columns].astype(jnp.float32) + scale * value
                    value = value - correction * streams[s, span, columns].astype(jnp.float32)
                    cotangent[later, :, columns] = value.astype(jnp.bfloat16)
            for columns in chunks(rank):
                share[:, columns] = dot(left[...], right[:, columns], ((0,), (0,)))
            hand_out(me, s, starts)

    by_section(plan, weights, body)


def on_device(node_table, tiles, neighbours, distances, proj, upstream):
    sections, replicas = lax.axis_size("section"), lax.axis_size("dp")
    micro_count, row_count, near = distances.shape
    nodes, width = node_table.shape
    rank = proj.shape[2]
    points = micro_count * row_count
    plan = Plan(sections, replicas, points)
    rows, unit, block = plan.rows, plan.unit, width // replicas
    me = lax.axis_index("section")

    in_vmem = pl.BlockSpec(memory_space=pltpu.VMEM)
    anywhere = pl.BlockSpec(memory_space=pl.ANY)
    bf16, f32 = jnp.bfloat16, jnp.float32
    in_hbm = functools.partial(pltpu.with_memory_space_constraint, memory_space=pltpu.HBM)
    flat_upstream = upstream.reshape(points, width)
    limit = pltpu.CompilerParams(vmem_limit_bytes=LIMIT)
    packs = [pltpu.VMEM((2 * near, points), f32)]
    if plan.relayed:
        packs += [pltpu.VMEM((points // 2, width), bf16)] * 2
    arrays = (tiles, neighbours.transpose(0, 2, 1), distances.transpose(0, 2, 1))
    prepare = pl.pallas_call(
        functools.partial(prepare_kernel, plan),
        out_shape=tuple(packs),
        in_specs=[anywhere] * 4,
        out_specs=(in_vmem,) * len(packs),
        scratch_shapes=[pltpu.VMEM(array.shape, array.dtype) for array in arrays] + [pltpu.SemaphoreType.DMA((5,))],
        compiler_params=limit,
        name="prepare",
    )
    small, *halves = prepare(*map(in_hbm, (*arrays, flat_upstream)))

    def part_of(array, axis, j):
        if plan.parts == 1:
            return array
        part = sum(jnp.where(me == section, plan.units_of(section)[j][1], 0) for section in range(sections))
        return lax.dynamic_slice_in_dim(array, part * unit, unit, axis)

    def unit_route(j):
        return lambda section, replica: (section, replica ^ plan.source_mask(section, j))

    def small_route(j):
        if plan.parts > 1 or j > 0:
            return unit_route(j)
        last = sections - 1
        return lambda section, replica: (last - section, replica ^ plan.source_mask(last - section, j))

    def relay_route(section, replica):
        return sections - 1 - section, replica ^ (1 << plan.shared[1 - section])

    weights = [in_hbm(proj)]
    for turn in range(1, sections):
        weights.append(permute(proj, plan, lambda section, replica: ((section - turn) % sections, replica)))
    if plan.relayed:
        arrived = []
        for j in range(2):
            arrived.append(permute(halves[j], plan, unit_route(0)))
        near = permute(small, plan, small_route(0))
        across = permute(near, plan, relay_route)
        arrived.append(permute(arrived[0], plan, relay_route))
        arrived.insert(2, halves[0])
        small_units = [near, across, small]
    else:
        arrived = [permute(part_of(flat_upstream, 0, j), plan, unit_route(j)) for j in range(plan.units)]
        small_units = [permute(part_of(small, 1, j), plan, small_route(j)) for j in range(plan.units)]

    formed = plan.blocks * block if block % 128 == 0 else width
    load = pl.pallas_call(
        functools.partial(load_kernel, plan),
        out_shape=(
            pltpu.VMEM((nodes, width), bf16),
            pltpu.VMEM((width, rank) if sections == 2 else (sections, width, rank), bf16),
        ),
        in_specs=[anywhere] * (1 + plan.loads),
        out_specs=(in_vmem,) * 2,
        scratch_shapes=[pltpu.SemaphoreType.DMA((1 + plan.loads,))],
        compiler_params=limit,
        name="load",
    )
    forward = pl.pallas_call(
        functools.partial(forward_kernel, plan),
        out_shape=(
            pltpu.VMEM((sections, rows, width), bf16),
            pltpu.VMEM((sections, rows, rank), bf16),
            pltpu.VMEM((sections, rows, rank), f32),
            pltpu.VMEM((sections, rows, 128), f32),
        ),
        in_specs=[in_vmem] * (len(small_units) + 1 + plan.held),
        out_specs=(in_vmem,) * 4,
        scratch_shapes=[pltpu.VMEM((2 * nodes, width), bf16), pltpu.VMEM((rows, 128), f32)],
        cost_estimate=pl.CostEstimate(
            flops=4 * sections * rows * width * rank, bytes_accessed=6 * width * rank, transcendentals=rows * rank
        ),
        compiler_params=limit,
        name="forward",
    )
    table, held = load(in_hbm(node_table), *weights[: plan.loads])
    held = [held, weights[1].reshape(width, rank)] if sections == 2 else [held]
    streams, hiddens, inputs, scales = forward(*small_units, table, *held)
    cuts = [(arrived, 0, rows)]
    outs = ()
    for given, low, count in cuts:
        last = low + count == rows
        shapes = [pltpu.VMEM((plan.blocks, block, rank), f32)]
        if sections > 1:
            shapes.append(pltpu.VMEM((sections - 1, plan.blocks, block, rank), bf16 if last else f32))
        backward = pl.pallas_call(
            functools.partial(backward_kernel, plan, len(given), low, count),
            out_shape=tuple(shapes),
            in_specs=[in_vmem] * (len(given) + 4 + plan.held + len(outs)),
            out_specs=(in_vmem,) * len(shapes),
            scratch_shapes=[
                pltpu.VMEM((2, count, width), bf16),
                pltpu.VMEM((count, rank), bf16),
                pltpu.VMEM((2 * count, formed), bf16),
                pltpu.VMEM((2 * count, rank), bf16),
                pltpu.VMEM((formed, rank), f32),
            ],
            cost_estimate=pl.CostEstimate(
                flops=6 * sections * count * width * rank, bytes_accessed=6 * width * rank, transcendentals=0
            ),
            compiler_params=limit,
        )
        outs = backward(*given, streams, hiddens, inputs, scales, *held, *outs)

    def split_sum(total, came):
        half = total.shape[0] // 2
        return pl.pallas_call(
            split_sum_kernel,
            out_shape=(pltpu.VMEM((half, block, rank), f32), pltpu.VMEM((half, block, rank), bf16)),
            in_specs=[in_vmem] * 2,
            out_specs=(in_vmem,) * 2,
            compiler_params=limit,
        )(total, pltpu.with_memory_space_constraint(came, pltpu.VMEM))

    def swap(array, turn):
        return permute(array, plan, lambda section, replica: ((section + turn) % sections, replica))

    total = outs[0]
    if sections == 2:
        came = swap(outs[1][0], 1)
    else:
        for turn in range(1, sections):
            total = total + swap(outs[1][turn - 1], turn).astype(f32)
    for stage in range(len(plan.summed)):

        def route(section, replica):
            return section, replica ^ (1 << plan.order(section)[stage])

        if sections == 2:
            total, leaving = split_sum(total, came)
        else:
            half = total.shape[0] // 2
            total, leaving = total[:half], total[half:].astype(bf16)
        came = permute(leaving, plan, route)
        if sections != 2:
            total = total + came.astype(f32)
    factor = 1.0 / math.sqrt(points * replicas)
    if sections != 2:
        return total * factor
    return pl.pallas_call(
        functools.partial(finish_kernel, factor),
        out_shape=jax.ShapeDtypeStruct(total.shape, f32),
        in_specs=[in_vmem] * 2,
        out_specs=anywhere,
        scratch_shapes=[pltpu.VMEM(total.shape, f32), pltpu.SemaphoreType.DMA((PARTS,))],
        compiler_params=limit,
        name="finish",
    )(total, pltpu.with_memory_space_constraint(came, pltpu.VMEM))


def finish_kernel(factor, total, came, out, held, sem):
    size = total.shape[1] // PARTS
    copies = []
    for i in range(PARTS):
        rows = pl.ds(i * size, size)
        held[:, rows, :] = (total[:, rows, :] + came[:, rows, :].astype(jnp.float32)) * factor
        copies.append(pltpu.make_async_copy(held.at[:, rows], out.at[:, rows], sem.at[i]))
        copies[-1].start()
    for copy in copies:
        copy.wait()


def split_sum_kernel(total, came, kept, leaving):
    half = kept.shape[0]
    kept[...] = total[:half] + came[:half].astype(jnp.float32)
    leaving[...] = (total[half:] + came[half:].astype(jnp.float32)).astype(jnp.bfloat16)


def solution(mesh):
    return jax.shard_map(
        on_device,
        mesh=mesh,
        in_specs=(
            P(),
            P(None, "dp"),
            P(None, "dp", None),
            P(None, "dp", None),
            P("section", None, None),
            P(None, "dp", None),
        ),
        out_specs=P("section", "dp", None),
        check_vma=False,
    )
```
